128 devices in a mesh: lat: 8 (over z, core), lon: 16 (over y, x).
Axes of the slice: x: 4, y: 4, z: 4, core: 2. Of those that a mesh axis runs over, the one named last changes fastest.
Arguments:
- sigma: float32 [4, 1024, 2048], P(None, 'lat', 'lon'), may hold values from 0.5 to 2
- east_coef: float32 [4, 1024, 2048], P(None, 'lat', 'lon'), may hold values from 0.04 to 0.24
- north_coef: float32 [4, 1024, 2048], P(None, 'lat', 'lon'), may hold values from 0.04 to 0.24
- mask: int32 [4, 1024, 2048], P(None, 'lat', 'lon'), may hold values 0 or 1
- innovations: float32 [16384, 128], P(('lat', 'lon')), may hold values from -6 to 6
- cells: int32 [16384, 128], P(('lat', 'lon')), may hold values from 0 to 65535
- owner: int32 [16384, 1], P(('lat', 'lon')), may hold values from 0 to 127; in each aligned block of 128 rows (0 to 127, 128 to 255, ...) at most 2 rows name the same one
- obs_weights: float32 [16384, 128, 128], P(('lat', 'lon')), may hold values from 0 to 4, as said below
Outputs:
- increment: float32 [4, 1024, 2048], P(None, 'lat', 'lon')
- residual: float32 [4, 1024, 2048], P(None, 'lat', 'lon')
The draws below stay inside these ranges and needn't reach their ends.
Inputs may be any that keep to these rules, and one draw needn't show every extreme that they name: `owner`: within the 128 blocks held by one device, no tile is named by more than 2 blocks, a bound that some block reaches. `obs_weights`: each block is symmetric and positive definite.
All inputs are finite; a program needn't handle non-finite values. No bound on the sum of `mask` on one device may be relied on, other than what follows from the above.
Results may differ from the reference program's by a relative error of at most 0.0003.
Values sent between devices are 32-bit elements; how exact they have to be, the bound alone decides.
A program may use at most 128 MiB of HBM per device.

```python
import math
import jax
import jax.numpy as jnp
import numpy as np
from jax import lax

LEVELS = 4
TILE_LAT = 128
TILE_LON = 128
BLOCKS_DEV = 128
BLOCK_OBS = 128
PASSES = 5
ITERS = 2
MOST = 2
NLAT = 1024
NLON = 2048
BLOCKS = 16384
CELLS = 65536
N_LON = 16
DEVICES = 128


def draw_obs_weights(key, part):
    key_place = jax.random.fold_in(key, 11)
    key_scale = jax.random.fold_in(key, 12)
    key_extra = jax.random.fold_in(key, 13)
    positions = jax.random.uniform(key_place, (BLOCKS, BLOCK_OBS), jnp.float32) * BLOCK_OBS
    log_scale = jax.random.uniform(key_scale, (BLOCKS, BLOCK_OBS), jnp.float32, -0.7, 0.7)
    length_scale = 6.0
    nugget = jax.random.uniform(key_extra, (BLOCKS, BLOCK_OBS), jnp.float32, 0.2, 0.6)
    distance = jnp.abs(positions[:, :, None] - positions[:, None, :])
    kernel = 0.5 * jnp.exp(log_scale[:, :, None] + log_scale[:, None, :] - distance / length_scale)
    identity = jnp.eye(BLOCK_OBS, dtype=jnp.float32)
    return kernel + identity[None, :, :] * nugget[:, :, None]


def plant(array, stream_key, smallest, top_value):
    longest = array.shape.index(max(array.shape))
    spots = []
    for shift in (0, 1):
        where = [jax.random.randint(jax.random.fold_in(stream_key, axis), (), 0, length) for axis, length in enumerate(array.shape)]
        where[longest] = (where[longest] + shift) % array.shape[longest]
        spots.append(tuple(where))
    return array.at[spots[0]].set(smallest).at[spots[1]].set(top_value)


def shard_levels(rng, extent, shards, low, high):
    loudness = 1.0
    for dim, blocks in shards:
        draws = jax.random.uniform(jax.random.fold_in(jax.random.fold_in(rng, 6), dim), (blocks,), jnp.float32, low / len(shards), high / len(shards))
        loudness = loudness * jnp.repeat(jnp.exp(draws), extent[dim] // blocks).reshape((-1,) + (1,) * (len(extent) - 1 - dim))
    return loudness


def routed_block(rng, own, number, rows, amount, top, reach, skew):
    ranking = jax.random.permutation(rng, amount)
    heavy_load, ordinary = shares(amount, rows * top, reach, skew, True), shares(amount, rows * top, reach, skew, False)
    places = jnp.arange(amount)

    def named(lengths, rotation):
        used = int((lengths > 0).sum())
        fixed = max(1, used // 4)
        passed = fixed + (places - fixed + rotation * (used - fixed)) % max(1, amount - fixed)
        return jnp.zeros((amount,), jnp.int32).at[ranking[jnp.where(places < fixed, places, passed)]].set(jnp.asarray(lengths, jnp.int32))

    lengths = jnp.where(number % 4 == 0, named(heavy_load, number // 4), named(ordinary, number - number // 4 - 1))
    mixed = jax.random.permutation(jax.random.fold_in(own, 3), amount)
    donor, sink = mixed[0:amount // 2 * 2:2], mixed[1:amount // 2 * 2:2]
    room = jnp.minimum(lengths[donor] - 1, reach - lengths[sink]) // 2
    room = jnp.where((donor == ranking[0]) | (sink == ranking[0]) | (lengths[sink] == 0), 0, jnp.maximum(room, 0))
    passed = jax.random.randint(jax.random.fold_in(own, 4), (amount // 2,), 0, 1 << 20) % (room + 1)
    lengths = lengths.at[donor].add(-passed).at[sink].add(passed)
    members = jnp.searchsorted(jnp.cumsum(lengths), jnp.arange(rows * top), side="right").astype(jnp.int32)
    listing = members.reshape(top, rows).T
    listing = listing[jax.random.permutation(jax.random.fold_in(own, 1), rows)]
    rotation = jax.random.randint(jax.random.fold_in(own, 2), (rows, 1), 0, top)
    return jnp.take_along_axis(listing, (jnp.arange(top)[None, :] + rotation) % top, axis=1)


def shares(number_of, total, most, skew, full):
    portions = [(1 << 20) // math.isqrt(grade ** skew) + 1 for grade in range(1, number_of + 1)]
    largest = most if full else min(most, max(-(-total // number_of), total * portions[0] // sum(portions)))
    least = 1 if total - largest >= number_of - 1 else 0
    holding, rest = [largest] + [least] * (number_of - 1), total - largest - least * (number_of - 1)
    while rest > 0:
        movable = [i for i in range(1, number_of) if holding[i] < largest] or [i for i in range(1, number_of) if holding[i] < most]
        mass, left = sum([portions[i] for i in movable]), rest
        for i in movable:
            extra = min(most - holding[i], max(1, left * portions[i] // mass), rest)
            holding[i] = holding[i] + extra
            rest = rest - extra
    return np.array(holding)


def scatter_about(key, extent, deviation, limit, split=(), kind=jnp.bfloat16):
    entries = deviation * jax.random.normal(key, extent, jnp.float32)
    if split:
        entries = entries * shard_levels(key, extent, split, -0.22, 0.18)
    return jnp.clip(entries, -limit, limit).astype(kind)


def setup_inputs(seed: int = 0) -> dict:
    splits = jax.random.split(jax.random.key(seed), 9)
    sigma = jnp.clip(jnp.exp(math.log(2.0) - 1.3862944 * jax.random.uniform(splits[0], (LEVELS, NLAT, NLON), jnp.float32) ** shard_levels(splits[0], (LEVELS, NLAT, NLON), ((1, 8), (2, 16)), -0.2, 0.2)), 0.5, 2.0)
    east_coef = jnp.clip(0.04 + 0.19999999552965164 * jax.random.uniform(splits[1], (LEVELS, NLAT, NLON), jnp.float32) ** shard_levels(splits[1], (LEVELS, NLAT, NLON), ((1, 8), (2, 16)), -0.2, 0.2), 0.04, 0.24)
    north_coef = jnp.clip(0.04 + 0.19999999552965164 * jax.random.uniform(splits[2], (LEVELS, NLAT, NLON), jnp.float32) ** shard_levels(splits[2], (LEVELS, NLAT, NLON), ((1, 8), (2, 16)), -0.2, 0.2), 0.04, 0.24)
    mask = plant((jax.random.randint(splits[3], (LEVELS, NLAT, NLON), 0, 10) < 9).astype(jnp.int32), jax.random.fold_in(splits[3], 1), 0, 1)
    innovations = scatter_about(splits[4], (BLOCKS, BLOCK_OBS), 1.0, 6.0, ((0, 128),), jnp.float32)
    cells = plant(jax.random.randint(splits[5], (BLOCKS, BLOCK_OBS), 0, CELLS), jax.random.fold_in(splits[5], 1), 0, CELLS - 1).astype(jnp.int32)
    owner_keys = jax.random.split(jax.random.fold_in(splits[6], 1), BLOCKS // BLOCKS_DEV)
    owner_turns = jax.random.permutation(jax.random.fold_in(splits[6], 3), BLOCKS // BLOCKS_DEV)
    owner = jax.vmap(lambda own, number: routed_block(jax.random.fold_in(splits[6], 2), own, number, BLOCKS_DEV, DEVICES, 1, MOST, 2))(owner_keys, owner_turns).reshape((BLOCKS, 1))
    obs_weights = draw_obs_weights(jax.random.fold_in(splits[8], 71), 0)
    return dict(sigma=sigma, east_coef=east_coef, north_coef=north_coef, mask=mask, innovations=innovations, cells=cells, owner=owner, obs_weights=obs_weights)


def face_weights(mask, east_coef, north_coef):
    land = mask.astype(jnp.float32)
    east = east_coef * land * jnp.roll(land, -1, 2)
    west = jnp.roll(east, 1, 2)
    upper = jnp.concatenate([land[:, 1:], jnp.zeros_like(land[:, :1])], 1)
    north = north_coef * land * upper
    south = jnp.concatenate([jnp.zeros_like(north[:, :1]), north[:, :-1]], 1)
    return east, west, north, south


def diffuse(field, weights):
    east, west, north, south = weights
    above = jnp.concatenate([field[:, 1:], jnp.zeros_like(field[:, :1])], 1)
    below = jnp.concatenate([jnp.zeros_like(field[:, :1]), field[:, :-1]], 1)
    result = field + east * (jnp.roll(field, -1, 2) - field) + west * (jnp.roll(field, 1, 2) - field)
    return result + north * (above - field) + south * (below - field)


def smooth(field, weights):
    for sweep in range(PASSES):
        field = diffuse(field, weights)
    return field


def reference(sigma, east_coef, north_coef, mask, innovations, cells, owner, obs_weights):
    weights = face_weights(mask, east_coef, north_coef)
    target = owner[:, 0].astype(jnp.int32)
    lat_tile = target // N_LON
    lon_tile = target % N_LON
    level = cells // (TILE_LAT * TILE_LON)
    row_index = (cells // TILE_LON) % TILE_LAT + lat_tile[:, None] * TILE_LAT
    col_index = cells % TILE_LON + lon_tile[:, None] * TILE_LON
    flat = ((level * NLAT + row_index) * NLON + col_index).astype(jnp.int32)

    def adjoint(values):
        total = jnp.zeros((LEVELS * NLAT * NLON,), jnp.float32).at[flat.reshape(-1)].add(values.reshape(-1))
        return total.reshape(LEVELS, NLAT, NLON)

    def weigh(values):
        return jnp.einsum("kij,kj->ki", obs_weights, values, precision=lax.Precision.HIGHEST)

    def hessian(direction):
        field = sigma * smooth(direction, weights)
        seen = field.reshape(-1)[flat]
        return direction + smooth(sigma * adjoint(weigh(seen)), weights)

    right = smooth(sigma * adjoint(weigh(innovations)), weights)
    solution = jnp.zeros_like(right)
    residual = right
    direction = right
    norm_now = jnp.sum(residual * residual)
    for sweep in range(ITERS):
        image = hessian(direction)
        alpha = norm_now / jnp.sum(direction * image)
        solution = solution + alpha * direction
        residual = residual - alpha * image
        norm_next = jnp.sum(residual * residual)
        direction = residual + (norm_next / norm_now) * direction
        norm_now = norm_next
    increment = sigma * smooth(solution, weights)
    return increment, residual
```

```python
import functools

import jax
import jax.numpy as jnp
from jax import lax
from jax.experimental import pallas as pl
from jax.experimental.pallas import tpu as pltpu
from jax.sharding import PartitionSpec as P

PASSES = 5
EDGE = 16
GROUP = 8
VMEM = pl.BlockSpec(memory_space=pltpu.VMEM)
LIMIT = pltpu.CompilerParams(vmem_limit_bytes=48 * 1024 * 1024)


def split(value):
    high = value.astype(jnp.bfloat16)
    low = (value - high.astype(jnp.float32)).astype(jnp.bfloat16)
    return high, low


def places(cells):
    line = cells >> 7
    return line & 255, ((line >> 8) << 7) + (cells & 127)


def hits(numbers, width):
    lines = lax.broadcasted_iota(jnp.int32, (256, width), 0)
    return lines == numbers


def scatter_kernel(cells_ref, value_ref, sigma_ref, out_ref, total):
    total[...] = jnp.zeros_like(total)
    width = cells_ref.shape[1]

    def step(group, carry):
        start = pl.multiple_of(group * GROUP, GROUP)
        row, column = places(cells_ref[pl.ds(start, GROUP), :])
        value = value_ref[pl.ds(start, GROUP), :]
        high = value.astype(jnp.bfloat16).astype(jnp.float32)
        low = value - high
        left, right = [], []
        for item in range(GROUP):
            row_hit = hits(row[item : item + 1], width)
            column_hit = hits(column[item : item + 1], width)
            spread = [jnp.where(row_hit, part[item : item + 1], 0.0) for part in (high, low)]
            left.append(jnp.concatenate(spread, 0).astype(jnp.bfloat16))
            right.append(jnp.where(column_hit, 1.0, 0.0).astype(jnp.bfloat16))
        total[...] += lax.dot_general(
            jnp.concatenate(left, 1),
            jnp.concatenate(right, 1),
            (((1,), (1,)), ((), ())),
            preferred_element_type=jnp.float32,
        )
        return carry

    lax.fori_loop(0, cells_ref.shape[0] // GROUP, step, 0)
    field = total[0:256] + total[256:512]
    out_ref[0:256] = field[:, 0:128] * sigma_ref[0:256]
    out_ref[256:512] = field[:, 128:256] * sigma_ref[256:512]


def gather_kernel(cells_ref, field_ref, out_ref, turned):
    square = jnp.concatenate([field_ref[0:256], field_ref[256:512]], 1).T
    high, low = split(square)
    turned[0:256] = high
    turned[256:512] = low
    width = cells_ref.shape[1]

    def step(group, carry):
        start = pl.multiple_of(group * GROUP, GROUP)
        row, column = places(cells_ref[pl.ds(start, GROUP), :])
        right = [
            jnp.where(hits(row[item : item + 1], width), 1.0, 0.0).astype(jnp.bfloat16)
            for item in range(GROUP)
        ]
        found = jnp.dot(
            turned[...], jnp.concatenate(right, 1), preferred_element_type=jnp.float32
        )
        found = found[0:256] + found[256:512]
        rows = []
        for item in range(GROUP):
            part = found[:, item * width : (item + 1) * width]
            part = jnp.where(hits(column[item : item + 1], width), part, 0.0)
            rows.append(jnp.sum(part, 0, keepdims=True))
        out_ref[pl.ds(start, GROUP), :] = jnp.concatenate(rows, 0)
        return carry

    lax.fori_loop(0, cells_ref.shape[0] // GROUP, step, 0)


def scatter(cells, value, sigma):
    return pl.pallas_call(
        scatter_kernel,
        out_shape=jax.ShapeDtypeStruct(sigma.shape, jnp.float32),
        in_specs=[VMEM] * 3,
        out_specs=VMEM,
        scratch_shapes=[pltpu.VMEM((512, 256), jnp.float32)],
        compiler_params=LIMIT,
        name="scatter",
    )(cells, value, sigma)


def gather(cells, field):
    return pl.pallas_call(
        gather_kernel,
        out_shape=jax.ShapeDtypeStruct(cells.shape, jnp.float32),
        in_specs=[VMEM] * 2,
        out_specs=VMEM,
        scratch_shapes=[pltpu.VMEM((512, 256), jnp.bfloat16)],
        compiler_params=LIMIT,
        name="gather",
    )(cells, field)


def faces_kernel(land_ref, east_ref, north_ref, out_ref):
    for level in range(land_ref.shape[0]):
        land = land_ref[level]
        rows, columns = land.shape
        east = east_ref[level] * land * pltpu.roll(land, columns - 1, 1)
        north = north_ref[level] * land * pltpu.roll(land, rows - 1, 0)
        out_ref[0, level] = east
        out_ref[1, level] = pltpu.roll(east, 1, 1)
        out_ref[2, level] = north
        out_ref[3, level] = pltpu.roll(north, 1, 0)


def faces(land, east, north):
    return pl.pallas_call(
        faces_kernel,
        out_shape=jax.ShapeDtypeStruct((4,) + land.shape, jnp.float32),
        in_specs=[VMEM] * 3,
        out_specs=VMEM,
        compiler_params=LIMIT,
        name="faces",
    )(land, east, north)


def smooth_kernel(twice, field_ref, faces_ref, sigma_ref, *outs_and_work):
    outs, work = outs_and_work[:-1], outs_and_work[-1]
    levels, rows, columns = field_ref.shape
    tile_rows, tile_columns = sigma_ref.shape[1:]

    def one_pass(level, source):
        x = source[level]
        total = x + faces_ref[0, level] * (pltpu.roll(x, columns - 1, 1) - x)
        total += faces_ref[1, level] * (pltpu.roll(x, 1, 1) - x)
        total += faces_ref[2, level] * (pltpu.roll(x, rows - 1, 0) - x)
        total += faces_ref[3, level] * (pltpu.roll(x, 1, 0) - x)
        work[level] = total

    def per_level(level, carry):
        one_pass(level, field_ref)
        for sweep in range(PASSES - 1):
            one_pass(level, work)
        outs[0][level] = work[level, 0:tile_rows, 0:tile_columns]
        if twice:
            for sweep in range(PASSES):
                one_pass(level, work)
            outs[1][level] = sigma_ref[level] * work[level, 0:tile_rows, 0:tile_columns]
        return carry

    lax.fori_loop(0, levels, per_level, 0)


def smooth(field, weights, sigma, twice):
    shape = jax.ShapeDtypeStruct(sigma.shape, jnp.float32)
    return pl.pallas_call(
        functools.partial(smooth_kernel, twice),
        out_shape=(shape,) * (2 if twice else 1),
        in_specs=[VMEM] * 3,
        out_specs=(VMEM,) * (2 if twice else 1),
        scratch_shapes=[pltpu.VMEM(field.shape, jnp.float32)],
        compiler_params=LIMIT,
        name="smooth",
    )(field, weights, sigma)


def ring(axis):
    count = lax.axis_size(axis)
    forward = [(i, (i + 1) % count) for i in range(count)]
    return forward, [(target, source) for source, target in forward]


def extend(block):
    rows, columns = block.shape[-2:]
    forward, backward = ring("lat")
    north = lax.ppermute(block[..., :EDGE, :], "lat", backward)
    south = lax.ppermute(block[..., rows - EDGE :, :], "lat", forward)
    block = jnp.concatenate([block, north, south], -2)
    forward, backward = ring("lon")
    east = lax.ppermute(block[..., :EDGE], "lon", backward)
    west = lax.ppermute(block[..., columns - EDGE :], "lon", forward)
    between = jnp.zeros(block.shape[:-1] + (columns - 2 * EDGE,), jnp.float32)
    return jnp.concatenate([block, east, between, west], -1)


def body(sigma, east_coef, north_coef, mask, innovations, cells, owner, obs_weights):
    devices = lax.axis_size("lat") * lax.axis_size("lon")
    held, width = cells.shape
    capacity = 2
    slots = devices * capacity
    levels, rows, columns = sigma.shape

    target = owner[:, 0]
    order = jnp.arange(held, dtype=jnp.int32)
    before = (target[:, None] == target[None, :]) & (order[None, :] < order[:, None])
    rank = jnp.sum(before.astype(jnp.int32), axis=1)
    position = target * capacity + rank
    placing = (jnp.arange(slots, dtype=jnp.int32)[:, None] == position[None, :]).astype(jnp.float32)

    def to_slots(blocks):
        return jnp.dot(placing, blocks, precision=lax.Precision.HIGHEST)

    def weigh(values):
        return jnp.einsum("kij,kj->ki", obs_weights, values, precision=lax.Precision.HIGHEST)

    def exchange(parcel):
        arrived = lax.all_to_all(
            parcel.reshape(devices, -1, width), ("lat", "lon"), split_axis=0, concat_axis=0, tiled=True
        )
        return arrived.reshape(slots, -1, width)

    stacked = extend(jnp.stack([mask.astype(jnp.float32), east_coef, north_coef]))
    line = lax.broadcasted_iota(jnp.int32, stacked.shape[2:], 0)
    line = jnp.where(line < rows + EDGE, line, line - rows - 2 * EDGE)
    line = lax.axis_index("lat") * rows + line
    inside = (line >= 0) & (line < rows * lax.axis_size("lat"))
    land = jnp.where(inside, stacked[0], 0.0)
    weights = faces(land, stacked[1], stacked[2])
    flat_sigma = sigma.reshape(levels * rows, columns)

    first = jnp.stack([to_slots(cells.astype(jnp.float32)), to_slots(weigh(innovations))], 1)
    first = exchange(first)
    here = first[:, 0].astype(jnp.int32)
    value = first[:, 1]

    def spread(value, twice):
        field = scatter(here, value, flat_sigma).reshape(sigma.shape)
        return smooth(extend(field), weights, sigma, twice)

    def seen(field):
        back = exchange(gather(here, field.reshape(flat_sigma.shape))).reshape(slots, width)
        values = jnp.dot(placing.T, back, precision=lax.Precision.HIGHEST)
        return exchange(to_slots(weigh(values))).reshape(slots, width)

    base, base_field = spread(value, True)
    once, once_field = spread(seen(base_field), True)
    (again,) = spread(seen(once_field), False)

    sums = jnp.stack(
        [jnp.sum(base * base), jnp.sum(base * once), jnp.sum(once * once), jnp.sum(once * again)]
    )
    s0, s1, s2, s3 = lax.psum(sums, ("lat", "lon"))
    alpha = s0 / (s0 + s1)
    rest = s1 / (s0 + s1)
    norm = alpha * (alpha * s2 - rest * s1)
    along = rest + norm / s0
    square = along * along * s0 - 2 * along * alpha * s1 + alpha * alpha * s2
    energy = along * along * s1 - 2 * along * alpha * s2 + alpha * alpha * s3
    step = norm / (square + energy)
    increment = (alpha + step * along) * base_field - step * alpha * once_field
    residual = (
        (rest - step * along) * base
        + (step * alpha - alpha - step * along) * once
        + step * alpha * again
    )
    return (increment, residual)


def solution(mesh):
    return jax.shard_map(
        body,
        mesh=mesh,
        in_specs=(
            P(None, "lat", "lon"),
            P(None, "lat", "lon"),
            P(None, "lat", "lon"),
            P(None, "lat", "lon"),
            P(("lat", "lon"), None),
            P(("lat", "lon"), None),
            P(("lat", "lon"), None),
            P(("lat", "lon"), None, None),
        ),
        out_specs=(P(None, "lat", "lon"), P(None, "lat", "lon")),
        check_vma=False,
    )
```

```python
import functools

import jax
import jax.numpy as jnp
from jax import lax
from jax.experimental import pallas as pl
from jax.experimental.pallas import tpu as pltpu
from jax.sharding import PartitionSpec as P

PASSES = 5
EDGE = 16
GROUP = 8
VMEM = pl.BlockSpec(memory_space=pltpu.VMEM)
LIMIT = pltpu.CompilerParams(vmem_limit_bytes=48 * 1024 * 1024)


def split(value):
    high = value.astype(jnp.bfloat16)
    low = (value - high.astype(jnp.float32)).astype(jnp.bfloat16)
    return high, low


def places(cells):
    line = cells >> 7
    return line & 255, ((line >> 8) << 7) + (cells & 127)


def hits(numbers, width):
    lines = lax.broadcasted_iota(jnp.int32, (256, width), 0)
    return lines == numbers


def scatter_kernel(cells_ref, value_ref, sigma_ref, out_ref, low_ref, high_ref, total):
    total[...] = jnp.zeros_like(total)
    width = cells_ref.shape[1]

    def step(group, carry):
        start = pl.multiple_of(group * GROUP, GROUP)
        row, column = places(cells_ref[pl.ds(start, GROUP), :])
        value = value_ref[pl.ds(start, GROUP), :]
        high = value.astype(jnp.bfloat16).astype(jnp.float32)
        low = value - high
        left, right = [], []
        for item in range(GROUP):
            row_hit = hits(row[item : item + 1], width)
            column_hit = hits(column[item : item + 1], width)
            spread = [jnp.where(row_hit, part[item : item + 1], 0.0) for part in (high, low)]
            left.append(jnp.concatenate(spread, 0).astype(jnp.bfloat16))
            right.append(jnp.where(column_hit, 1.0, 0.0).astype(jnp.bfloat16))
        total[...] += lax.dot_general(
            jnp.concatenate(left, 1),
            jnp.concatenate(right, 1),
            (((1,), (1,)), ((), ())),
            preferred_element_type=jnp.float32,
        )
        return carry

    lax.fori_loop(0, cells_ref.shape[0] // GROUP, step, 0)
    field = total[0:256] + total[256:512]
    out_ref[0:256] = field[:, 0:128] * sigma_ref[0:256]
    out_ref[256:512] = field[:, 128:256] * sigma_ref[256:512]
    for level in range(low_ref.shape[0]):
        flat = out_ref[level * 128 : level * 128 + 128].T
        low_ref[level] = flat[0:EDGE]
        high_ref[level] = flat[128 - EDGE : 128]


def gather_kernel(cells_ref, field_ref, out_ref, turned):
    square = jnp.concatenate([field_ref[0:256], field_ref[256:512]], 1).T
    high, low = split(square)
    turned[0:256] = high
    turned[256:512] = low
    width = cells_ref.shape[1]

    def step(group, carry):
        start = pl.multiple_of(group * GROUP, GROUP)
        row, column = places(cells_ref[pl.ds(start, GROUP), :])
        right = [
            jnp.where(hits(row[item : item + 1], width), 1.0, 0.0).astype(jnp.bfloat16)
            for item in range(GROUP)
        ]
        found = jnp.dot(
            turned[...], jnp.concatenate(right, 1), preferred_element_type=jnp.float32
        )
        found = found[0:256] + found[256:512]
        rows = []
        for item in range(GROUP):
            part = found[:, item * width : (item + 1) * width]
            part = jnp.where(hits(column[item : item + 1], width), part, 0.0)
            rows.append(jnp.sum(part, 0, keepdims=True))
        out_ref[pl.ds(start, GROUP), :] = jnp.concatenate(rows, 0)
        return carry

    lax.fori_loop(0, cells_ref.shape[0] // GROUP, step, 0)


def scatter(cells, value, sigma):
    return pl.pallas_call(
        scatter_kernel,
        out_shape=(jax.ShapeDtypeStruct(sigma.shape, jnp.float32),)
        + (jax.ShapeDtypeStruct((4, EDGE, 128), jnp.float32),) * 2,
        in_specs=[VMEM] * 3,
        out_specs=(VMEM,) * 3,
        scratch_shapes=[pltpu.VMEM((512, 256), jnp.float32)],
        compiler_params=LIMIT,
        name="scatter",
    )(cells, value, sigma)


def gather(cells, field):
    return pl.pallas_call(
        gather_kernel,
        out_shape=jax.ShapeDtypeStruct(cells.shape, jnp.float32),
        in_specs=[VMEM] * 2,
        out_specs=VMEM,
        scratch_shapes=[pltpu.VMEM((512, 256), jnp.bfloat16)],
        compiler_params=LIMIT,
        name="gather",
    )(cells, field)


def neighbours():
    lats, lons = lax.axis_size("lat"), lax.axis_size("lon")
    lat, lon = lax.axis_index("lat"), lax.axis_index("lon")
    steps = [(1, 0), (-1, 0), (0, 1), (0, -1), (1, 1), (1, -1), (-1, 1), (-1, -1)]
    return [(lax.rem(lat + a + lats, lats), lax.rem(lon + b + lons, lons)) for a, b in steps]


def swap_edges(field_ref, low_ref, high_ref, edges, send, receive):
    partners = neighbours()
    barrier = pltpu.get_barrier_semaphore()
    for partner in partners:
        pl.semaphore_signal(barrier, inc=1, device_id=partner, device_id_type=pl.DeviceIdType.MESH)
    pl.semaphore_wait(barrier, len(partners))
    rows = field_ref.shape[1]
    top = field_ref.at[:, rows - EDGE : rows, :]
    bottom = field_ref.at[:, 0:EDGE, :]
    sources = [top, bottom, high_ref, low_ref, top, top, bottom, bottom]
    landing = [1, 0, 3, 2, 7, 6, 5, 4]
    copies = []
    for number, partner in enumerate(partners):
        copy = pltpu.make_async_remote_copy(
            src_ref=sources[number],
            dst_ref=edges.at[landing[number]],
            send_sem=send.at[number],
            recv_sem=receive.at[landing[number]],
            device_id=partner,
            device_id_type=pl.DeviceIdType.MESH,
        )
        copy.start()
        copies.append(copy)
    return copies


def assemble(level, field_ref, edges):
    shape = (EDGE, field_ref.shape[2])
    lane = lax.broadcasted_iota(jnp.int32, shape, 1)

    def corner(east, west):
        inner = jnp.where(lane >= shape[1] - EDGE, edges[west, level], 0.0)
        return jnp.where(lane < EDGE, edges[east, level], inner)

    gap = jnp.zeros((shape[1] - 2 * EDGE, field_ref.shape[1]), jnp.float32)
    beside = jnp.concatenate([edges[2, level], gap, edges[3, level]], 0).T
    upper = jnp.concatenate([field_ref[level], beside], 1)
    north = jnp.concatenate([edges[0, level], corner(4, 5)], 1)
    south = jnp.concatenate([edges[1, level], corner(6, 7)], 1)
    return jnp.concatenate([upper, north, south], 0)


def faces_kernel(field_ref, low_ref, high_ref, out_ref, edges, send, receive):
    copies = swap_edges(field_ref, low_ref, high_ref, edges, send, receive)
    for copy in copies:
        copy.wait()
    levels = out_ref.shape[1]
    rows, columns = out_ref.shape[2:]
    tile_rows = field_ref.shape[1]
    line = lax.broadcasted_iota(jnp.int32, (rows, columns), 0)
    line = jnp.where(line < tile_rows + EDGE, line, line - tile_rows - 2 * EDGE)
    line = lax.axis_index("lat") * tile_rows + line
    inside = (line >= 0) & (line < tile_rows * lax.axis_size("lat"))

    def per_level(level, carry):
        land = jnp.where(inside, assemble(level, field_ref, edges), 0.0)
        east = assemble(levels + level, field_ref, edges)
        north = assemble(2 * levels + level, field_ref, edges)
        east = east * land * pltpu.roll(land, columns - 1, 1)
        north = north * land * pltpu.roll(land, rows - 1, 0)
        out_ref[0, level] = east
        out_ref[1, level] = pltpu.roll(east, 1, 1)
        out_ref[2, level] = north
        out_ref[3, level] = pltpu.roll(north, 1, 0)
        return carry

    lax.fori_loop(0, levels, per_level, 0)


def edge_scratch(levels, columns):
    return [
        pltpu.VMEM((8, levels, EDGE, columns), jnp.float32),
        pltpu.SemaphoreType.DMA((8,)),
        pltpu.SemaphoreType.DMA((8,)),
    ]


def faces(stacked):
    levels, rows, columns = stacked.shape
    low = jnp.swapaxes(stacked[:, :, :EDGE], 1, 2)
    high = jnp.swapaxes(stacked[:, :, columns - EDGE :], 1, 2)
    return pl.pallas_call(
        faces_kernel,
        out_shape=jax.ShapeDtypeStruct((4, levels // 3, rows + 2 * EDGE, 2 * columns), jnp.float32),
        in_specs=[VMEM] * 3,
        out_specs=VMEM,
        scratch_shapes=edge_scratch(levels, columns),
        compiler_params=remote(0),
        name="faces",
    )(stacked, low, high)


def remote(number):
    return pltpu.CompilerParams(
        vmem_limit_bytes=48 * 1024 * 1024, collective_id=number, has_side_effects=True
    )


def smooth_kernel(twice, field_ref, low_ref, high_ref, faces_ref, sigma_ref, *rest):
    if twice:
        outs, rest = rest[:2], rest[2:]
    else:
        base_ref, once_ref = rest[:2]
        outs, rest = rest[2:4], rest[4:]
    work, edges, send, receive = rest
    levels, tile_rows, tile_columns = field_ref.shape
    rows, columns = work.shape[1:]
    copies = swap_edges(field_ref, low_ref, high_ref, edges, send, receive)
    for copy in copies:
        copy.wait()

    def one_pass(level, x):
        total = x + faces_ref[0, level] * (pltpu.roll(x, columns - 1, 1) - x)
        total += faces_ref[1, level] * (pltpu.roll(x, 1, 1) - x)
        total += faces_ref[2, level] * (pltpu.roll(x, rows - 1, 0) - x)
        total += faces_ref[3, level] * (pltpu.roll(x, 1, 0) - x)
        work[level] = total

    def per_level(level, carry):
        one_pass(level, assemble(level, field_ref, edges))
        for sweep in range(PASSES - 1):
            one_pass(level, work[level])
        tile = work[level, 0:tile_rows, 0:tile_columns]
        outs[0][level] = tile
        if twice:
            for sweep in range(PASSES):
                one_pass(level, work[level])
            outs[1][level] = sigma_ref[level] * work[level, 0:tile_rows, 0:tile_columns]
            return carry
        base, once = base_ref[level], once_ref[level]
        products = (base * base, base * once, once * once, once * tile)
        return carry + jnp.concatenate([jnp.sum(p, 0, keepdims=True) for p in products], 0)

    sums = lax.fori_loop(0, levels, per_level, jnp.zeros((4, tile_columns), jnp.float32))
    if not twice:
        outs[1][...] = jnp.concatenate([sums, sums], 0)


def smooth(number, scattered, weights, sigma, bases=()):
    field, low, high = scattered
    twice = not bases
    shape = jax.ShapeDtypeStruct(sigma.shape, jnp.float32)
    levels, rows, columns = sigma.shape
    return pl.pallas_call(
        functools.partial(smooth_kernel, twice),
        out_shape=(shape, shape if twice else jax.ShapeDtypeStruct((8, columns), jnp.float32)),
        in_specs=[VMEM] * (5 + len(bases)),
        out_specs=(VMEM, VMEM),
        scratch_shapes=[pltpu.VMEM(weights.shape[1:], jnp.float32)] + edge_scratch(levels, columns),
        compiler_params=remote(number),
        name="smooth",
    )(field.reshape(sigma.shape), low, high, weights, sigma, *bases)


def everyone():
    lats, lons = lax.axis_size("lat"), lax.axis_size("lon")
    devices = lats * lons
    me = lax.axis_index("lat") * lons + lax.axis_index("lon")

    def partner(distance):
        other = lax.rem(me + distance, devices)
        return other, (other // lons, lax.rem(other, lons))

    barrier = pltpu.get_barrier_semaphore()

    def greet(distance, carry):
        pl.semaphore_signal(
            barrier, inc=1, device_id=partner(distance)[1], device_id_type=pl.DeviceIdType.MESH
        )
        return carry

    lax.fori_loop(1, devices, greet, 0)
    pl.semaphore_wait(barrier, devices - 1)
    return devices, me, partner


def total_kernel(part_ref, out_ref, landing, send, receive):
    devices, me, partner = everyone()

    def tell(distance, carry):
        pltpu.make_async_remote_copy(
            src_ref=part_ref,
            dst_ref=landing.at[distance - 1],
            send_sem=send,
            recv_sem=receive,
            device_id=partner(distance)[1],
            device_id_type=pl.DeviceIdType.MESH,
        ).start()
        return carry

    lax.fori_loop(1, devices, tell, 0)
    pltpu.make_async_copy(landing, landing, send).wait()
    pltpu.make_async_copy(landing, landing, receive).wait()
    out_ref[...] = jnp.sum(landing[...], 0) + part_ref[...]


def add_all(part):
    devices = lax.axis_size("lat") * lax.axis_size("lon")
    return pl.pallas_call(
        total_kernel,
        out_shape=jax.ShapeDtypeStruct(part.shape, jnp.float32),
        in_specs=[VMEM],
        out_specs=VMEM,
        scratch_shapes=[
            pltpu.VMEM((devices - 1,) + part.shape, jnp.float32),
            pltpu.SemaphoreType.DMA,
            pltpu.SemaphoreType.DMA,
        ],
        compiler_params=remote(4),
        name="total",
    )(part)


STEP = 16


def weigh_kernel(first, place_ref, value_ref, *rest):
    if first:
        cells_ref, rest = rest[0], rest[1:]
    weights_ref, out_ref, turned, weighted = rest
    number = pl.program_id(0)
    slots, held = out_ref.shape[0], turned.shape[1]
    place = lax.broadcasted_iota(jnp.int32, (slots, held), 0)

    @pl.when(number == 0)
    def _():
        if first:
            turned[...] = value_ref[...].T
        else:
            turned[...] = lax.dot_general(
                value_ref[...],
                jnp.where(place == place_ref[0:1], 1.0, 0.0),
                (((0,), (0,)), ((), ())),
                precision=lax.Precision.HIGHEST,
                preferred_element_type=jnp.float32,
            )

    values = turned[...]
    rows = []
    for item in range(STEP):
        column = values[:, item : item + 1]
        rows.append(jnp.sum(weights_ref[item] * column, 0, keepdims=True))
    weighted[pl.ds(pl.multiple_of(number * STEP, STEP), STEP), :] = jnp.concatenate(rows, 0)
    turned[...] = pltpu.roll(values, held - STEP, 1)

    @pl.when(number == pl.num_programs(0) - 1)
    def _():
        def to_slots(row, blocks):
            return jnp.dot(
                jnp.where(place == place_ref[row : row + 1], 1.0, 0.0),
                blocks,
                precision=lax.Precision.HIGHEST,
                preferred_element_type=jnp.float32,
            )

        if first:
            out_ref[...] = to_slots(1, cells_ref[...].astype(jnp.float32)) + to_slots(
                2, weighted[...]
            )
        else:
            out_ref[...] = to_slots(0, weighted[...])


def weigh(place, value, weights, cells=None):
    held, width = weights.shape[:2]
    devices = lax.axis_size("lat") * lax.axis_size("lon")
    first = cells is not None
    fixed = [place, value] + ([cells] if first else [])
    return pl.pallas_call(
        functools.partial(weigh_kernel, first),
        out_shape=jax.ShapeDtypeStruct((devices * (4 if first else 2), width), jnp.float32),
        grid=(held // STEP,),
        in_specs=[pl.BlockSpec(x.shape, lambda i: (0, 0)) for x in fixed]
        + [pl.BlockSpec((STEP, width, width), lambda i: (i, 0, 0))],
        out_specs=pl.BlockSpec((devices * (4 if first else 2), width), lambda i: (0, 0)),
        scratch_shapes=[
            pltpu.VMEM((width, held), jnp.float32),
            pltpu.VMEM((held, width), jnp.float32),
        ],
        compiler_params=LIMIT,
        name="weigh",
    )(*fixed, weights)


def body(sigma, east_coef, north_coef, mask, innovations, cells, owner, obs_weights):
    devices = lax.axis_size("lat") * lax.axis_size("lon")
    held, width = cells.shape
    capacity = 2
    slots = devices * capacity
    levels, rows, columns = sigma.shape

    target = owner[:, 0]
    order = jnp.arange(held, dtype=jnp.int32)
    before = (target[:, None] == target[None, :]) & (order[:, None] < order[None, :])
    rank = jnp.sum(before.astype(jnp.int32), axis=0)
    place = target * capacity
    place = jnp.stack([place + rank, 2 * place + rank, 2 * place + 2 + rank] + [rank] * 5)

    def exchange(parcel):
        return lax.all_to_all(
            parcel.reshape(devices, -1, width), ("lat", "lon"), split_axis=0, concat_axis=0, tiled=True
        )

    stacked = jnp.concatenate([mask.astype(jnp.float32), east_coef, north_coef])
    weights = faces(stacked)
    flat_sigma = sigma.reshape(levels * rows, columns)

    first = exchange(weigh(place, innovations, obs_weights, cells))
    here = first[:, 0:2].reshape(slots, width).astype(jnp.int32)
    value = first[:, 2:4].reshape(slots, width)

    def seen(field):
        back = exchange(gather(here, field.reshape(flat_sigma.shape))).reshape(slots, width)
        return exchange(weigh(place, back, obs_weights)).reshape(slots, width)

    base, base_field = smooth(1, scatter(here, value, flat_sigma), weights, sigma)
    once, once_field = smooth(
        2, scatter(here, seen(base_field), flat_sigma), weights, sigma
    )
    again, part = smooth(
        3, scatter(here, seen(once_field), flat_sigma), weights, sigma, (base, once)
    )
    sums = jnp.sum(add_all(part), 1)
    s0, s1, s2, s3 = sums[0], sums[1], sums[2], sums[3]
    alpha = s0 / (s0 + s1)
    rest = s1 / (s0 + s1)
    norm = alpha * (alpha * s2 - rest * s1)
    along = rest + norm / s0
    square = along * along * s0 - 2 * along * alpha * s1 + alpha * alpha * s2
    energy = along * along * s1 - 2 * along * alpha * s2 + alpha * alpha * s3
    step = norm / (square + energy)
    increment = (alpha + step * along) * base_field - step * alpha * once_field
    residual = (
        (rest - step * along) * base
        + (step * alpha - alpha - step * along) * once
        + step * alpha * again
    )
    return (increment, residual)


def solution(mesh):
    return jax.shard_map(
        body,
        mesh=mesh,
        in_specs=(
            P(None, "lat", "lon"),
            P(None, "lat", "lon"),
            P(None, "lat", "lon"),
            P(None, "lat", "lon"),
            P(("lat", "lon"), None),
            P(("lat", "lon"), None),
            P(("lat", "lon"), None),
            P(("lat", "lon"), None, None),
        ),
        out_specs=(P(None, "lat", "lon"), P(None, "lat", "lon")),
        check_vma=False,
    )
```

```python
import functools

import jax
import jax.numpy as jnp
from jax import lax
from jax.experimental import pallas as pl
from jax.experimental.pallas import tpu as pltpu
from jax.sharding import PartitionSpec as P

PASSES = 5
EDGE = 16
GROUP = 8
STEP = 16
MESH = pl.DeviceIdType.MESH
EXACT = lax.Precision.HIGHEST
VMEM = pl.BlockSpec(memory_space=pltpu.VMEM)


def split(value):
    high = value.astype(jnp.bfloat16)
    low = (value - high.astype(jnp.float32)).astype(jnp.bfloat16)
    return high, low


def places(cells):
    line = cells >> 7
    return line & 255, ((line >> 8) << 7) + (cells & 127)


def hits(numbers, width):
    lines = lax.broadcasted_iota(jnp.int32, (256, width), 0)
    return lines == numbers


def neighbours():
    lats, lons = lax.axis_size("lat"), lax.axis_size("lon")
    lat, lon = lax.axis_index("lat"), lax.axis_index("lon")
    steps = [(1, 0), (-1, 0), (0, 1), (0, -1), (1, 1), (1, -1), (-1, 1), (-1, -1)]
    return [(lax.rem(lat + a + lats, lats), lax.rem(lon + b + lons, lons)) for a, b in steps]


def greet_neighbours():
    partners = neighbours()
    barrier = pltpu.get_barrier_semaphore()
    for partner in partners:
        pl.semaphore_signal(barrier, inc=1, device_id=partner, device_id_type=MESH)
    pl.semaphore_wait(barrier, len(partners))


def swap_edges(field_ref, low_ref, high_ref, edges, send, receive):
    partners = neighbours()
    rows = field_ref.shape[1]
    top = field_ref.at[:, rows - EDGE : rows, :]
    bottom = field_ref.at[:, 0:EDGE, :]
    sources = [top, bottom, high_ref, low_ref, top, top, bottom, bottom]
    landing = [1, 0, 3, 2, 7, 6, 5, 4]
    copies = []
    for number in (0, 1, 4, 5, 6, 7, 2, 3):
        partner = partners[number]
        copy = pltpu.make_async_remote_copy(
            src_ref=sources[number],
            dst_ref=edges.at[landing[number]],
            send_sem=send.at[number],
            recv_sem=receive.at[landing[number]],
            device_id=partner,
            device_id_type=MESH,
        )
        copy.start()
        copies.append(copy)
    return copies


def assemble(level, field_ref, edges):
    shape = (EDGE, field_ref.shape[2])
    lane = lax.broadcasted_iota(jnp.int32, shape, 1)

    def corner(east, west):
        inner = jnp.where(lane >= shape[1] - EDGE, edges[west, level], 0.0)
        return jnp.where(lane < EDGE, edges[east, level], inner)

    gap = jnp.zeros((shape[1] - 2 * EDGE, field_ref.shape[1]), jnp.float32)
    beside = jnp.concatenate([edges[2, level], gap, edges[3, level]], 0).T
    upper = jnp.concatenate([field_ref[level], beside], 1)
    north = jnp.concatenate([edges[0, level], corner(4, 5)], 1)
    south = jnp.concatenate([edges[1, level], corner(6, 7)], 1)
    return jnp.concatenate([upper, north, south], 0)


def faces_kernel(field_ref, low_ref, high_ref, out_ref, edges, send, receive):
    greet_neighbours()
    for copy in swap_edges(field_ref, low_ref, high_ref, edges, send, receive):
        copy.wait()
    levels = out_ref.shape[1]
    rows, columns = out_ref.shape[2:]
    tile_rows = field_ref.shape[1]
    line = lax.broadcasted_iota(jnp.int32, (rows, columns), 0)
    line = jnp.where(line < tile_rows + EDGE, line, line - tile_rows - 2 * EDGE)
    line = lax.axis_index("lat") * tile_rows + line
    inside = (line >= 0) & (line < tile_rows * lax.axis_size("lat"))

    def per_level(level, carry):
        land = jnp.where(inside, assemble(level, field_ref, edges), 0.0)
        east = assemble(levels + level, field_ref, edges)
        north = assemble(2 * levels + level, field_ref, edges)
        east = east * land * pltpu.roll(land, columns - 1, 1)
        north = north * land * pltpu.roll(land, rows - 1, 0)
        out_ref[0, level] = east
        out_ref[1, level] = pltpu.roll(east, 1, 1)
        out_ref[2, level] = north
        out_ref[3, level] = pltpu.roll(north, 1, 0)
        return carry

    lax.fori_loop(0, levels, per_level, 0)


def edge_scratch(levels, columns):
    return [
        pltpu.VMEM((8, levels, EDGE, columns), jnp.float32),
        pltpu.SemaphoreType.DMA((8,)),
        pltpu.SemaphoreType.DMA((8,)),
    ]


def faces(stacked):
    levels, rows, columns = stacked.shape
    low = jnp.swapaxes(stacked[:, :, :EDGE], 1, 2)
    high = jnp.swapaxes(stacked[:, :, columns - EDGE :], 1, 2)
    return pl.pallas_call(
        faces_kernel,
        out_shape=jax.ShapeDtypeStruct((4, levels // 3, rows + 2 * EDGE, 2 * columns), jnp.float32),
        in_specs=[VMEM] * 3,
        out_specs=VMEM,
        scratch_shapes=edge_scratch(levels, columns),
        compiler_params=remote(0),
        name="faces",
    )(stacked, low, high)


def remote(number):
    return pltpu.CompilerParams(
        vmem_limit_bytes=48 * 1024 * 1024, collective_id=number, has_side_effects=True
    )


def everyone():
    lats, lons = lax.axis_size("lat"), lax.axis_size("lon")
    return lats * lons, lax.axis_index("lat") * lons + lax.axis_index("lon")


def where_is(device):
    lons = lax.axis_size("lon")
    return lax.div(device, lons), lax.rem(device, lons)


def greet_everyone():
    devices, me = everyone()
    barrier = pltpu.get_barrier_semaphore()

    def greet(distance, carry):
        partner = where_is(lax.rem(me + distance, devices))
        pl.semaphore_signal(barrier, inc=1, device_id=partner, device_id_type=MESH)
        return carry

    lax.fori_loop(1, devices, greet, 0)
    pl.semaphore_wait(barrier, devices - 1)


def push(source, target, send, receive, device):
    pltpu.make_async_remote_copy(
        src_ref=source,
        dst_ref=target,
        send_sem=send,
        recv_sem=receive,
        device_id=where_is(device),
        device_id_type=MESH,
    ).start()


def wait_for(ref, semaphore):
    pltpu.make_async_copy(ref, ref, semaphore).wait()


def gather_and_send(here, field_ref, turned, found_ref, back, send, receive):
    square = jnp.concatenate([field_ref[0:256], field_ref[256:512]], 1).T
    high, low = split(square)
    turned[0:256] = high
    turned[256:512] = low
    devices, me = everyone()
    ranks, width = here.shape[1:]
    batch = GROUP // ranks
    groups = devices // batch

    def group_of(turn):
        return lax.rem(lax.div(me, batch) + turn, groups)

    def send_group(turn):
        for item in range(batch):
            device = group_of(turn) * batch + item

            @pl.when(device != me)
            def _():
                push(found_ref.at[device], back.at[me], send, receive, device)

            @pl.when(device == me)
            def _():
                pltpu.make_async_copy(found_ref.at[device], back.at[device], receive).start()

    def step(turn, carry):
        start = group_of(turn) * batch
        places_of = [
            places(here[start + item // ranks, item % ranks : item % ranks + 1])
            for item in range(GROUP)
        ]
        right = [
            jnp.where(hits(row, width), 1.0, 0.0).astype(jnp.bfloat16) for row, _ in places_of
        ]
        found = jnp.dot(
            turned[...], jnp.concatenate(right, 1), preferred_element_type=jnp.float32
        )
        found = found[0:256] + found[256:512]
        for item in range(GROUP):
            part = found[:, item * width : (item + 1) * width]
            part = jnp.where(hits(places_of[item][1], width), part, 0.0)
            spot = item % ranks
            found_ref[start + item // ranks, spot : spot + 1] = jnp.sum(part, 0, keepdims=True)

        @pl.when(turn > 0)
        def _():
            send_group(turn - 1)

        return carry

    lax.fori_loop(0, groups, step, 0)
    send_group(groups - 1)
    wait_for(back, receive)


def weigh(turned, weights_ref, weighted):
    held = turned.shape[1]

    def step(number, carry):
        values = turned[...]
        start = pl.multiple_of(number * STEP, STEP)
        rows = []
        for item in range(STEP):
            column = values[:, item : item + 1]
            rows.append(jnp.sum(weights_ref[start + item] * column, 0, keepdims=True))
        weighted[pl.ds(start, STEP), :] = jnp.concatenate(rows, 0)
        turned[...] = pltpu.roll(values, held - STEP, 1)
        return carry

    lax.fori_loop(0, held // STEP, step, 0)


def scatter_arrivals(first, here, parcel, arrived, total, send, receive):
    devices, me = everyone()
    ranks, width = here.shape[1:]
    batch = GROUP // ranks
    groups = devices // batch
    mine = lax.div(me, batch)

    pltpu.make_async_copy(parcel.at[me], arrived.at[me], receive.at[mine]).start()

    def tell(distance, carry):
        device = lax.rem(me + distance, devices)
        push(parcel.at[device], arrived.at[me], send, receive.at[mine], device)
        return carry

    lax.fori_loop(1, devices, tell, 0)

    def step(turn, carry):
        group = lax.rem(mine + 2 * groups - 1 - turn, groups)
        start = group * batch
        wait_for(arrived.at[pl.ds(start, batch)], receive.at[group])
        left, right = [], []
        for item in range(GROUP):
            device, spot = start + item // ranks, item % ranks
            if first:
                cells = arrived[device, spot : spot + 1].astype(jnp.int32)
                here[device, spot : spot + 1] = cells
                value = arrived[device, ranks + spot : ranks + spot + 1]
            else:
                cells = here[device, spot : spot + 1]
                value = arrived[device, spot : spot + 1]
            row, column = places(cells)
            high = value.astype(jnp.bfloat16).astype(jnp.float32)
            row_hit = hits(row, width)
            spread = [jnp.where(row_hit, part, 0.0) for part in (high, value - high)]
            left.append(jnp.concatenate(spread, 0).astype(jnp.bfloat16))
            right.append(jnp.where(hits(column, width), 1.0, 0.0).astype(jnp.bfloat16))
        total[...] += lax.dot_general(
            jnp.concatenate(left, 1),
            jnp.concatenate(right, 1),
            (((1,), (1,)), ((), ())),
            preferred_element_type=jnp.float32,
        )
        return carry

    lax.fori_loop(0, groups, step, 0)


def phase_kernel(mode, *refs):
    first, last = mode == "first", mode == "last"
    place_ref, weights_hbm, faces_ref, sigma_ref = refs[:4]
    refs = refs[4:]
    if first:
        cells_ref, value_ref, smoothed, field_out, here = refs[:5]
        refs = refs[5:]
    elif last:
        here, seen_ref, base_ref, once_ref, smoothed, scale_out = refs[:6]
        refs = refs[6:]
    else:
        here, seen_ref, smoothed, field_out = refs[:4]
        refs = refs[4:]
    weights_ref, turned, weighted, parcel, arrived, total, field_ref, low, high, work = refs[:10]
    copied, send, receive, edges, edge_send, edge_receive = refs[10:16]
    refs = refs[16:]
    if not first:
        square, found, back, found_send, found_receive = refs[:5]
        refs = refs[5:]
    if last:
        part, parts, part_send, part_receive = refs

    load = pltpu.make_async_copy(weights_hbm, weights_ref, copied)
    load.start()
    greet_everyone()
    devices, me = everyone()
    ranks, width = here.shape[1:]
    held = turned.shape[1]
    number = lax.broadcasted_iota(jnp.int32, (devices, held), 0)

    def placing(rank):
        return jnp.where(number * ranks + rank == place_ref[0:1], 1.0, 0.0)

    if first:
        turned[...] = value_ref[...].T
    else:
        gather_and_send(here, seen_ref, square, found, back, found_send, found_receive)
        turned[...] = sum(
            lax.dot_general(
                back[:, rank, :],
                placing(rank),
                (((0,), (0,)), ((), ())),
                precision=EXACT,
                preferred_element_type=jnp.float32,
            )
            for rank in range(ranks)
        )
    load.wait()
    weigh(turned, weights_ref, weighted)
    for rank in range(ranks):
        chosen = placing(rank)
        if first:
            parcel[:, rank, :] = jnp.dot(
                chosen,
                cells_ref[...].astype(jnp.float32),
                precision=EXACT,
                preferred_element_type=jnp.float32,
            )
        parcel[:, (ranks if first else 0) + rank, :] = jnp.dot(
            chosen, weighted[...], precision=EXACT, preferred_element_type=jnp.float32
        )
    total[...] = jnp.zeros_like(total)
    scatter_arrivals(first, here, parcel, arrived, total, send, receive)

    field = total[0:256] + total[256:512]
    levels, tile_rows, tile_columns = field_ref.shape
    for level in range(levels):
        start, side = level * 128 % 256, level * 128 // 256 * 128
        tile = field[start : start + 128, side : side + 128] * sigma_ref[level]
        field_ref[level] = tile
        flat = tile.T
        low[level] = flat[0:EDGE]
        high[level] = flat[tile_columns - EDGE :]
    copies = swap_edges(field_ref, low, high, edges, edge_send, edge_receive)
    for copy in copies:
        copy.wait()
    rows, columns = work.shape[1:]

    def one_pass(level, x):
        result = x + faces_ref[0, level] * (pltpu.roll(x, columns - 1, 1) - x)
        result += faces_ref[1, level] * (pltpu.roll(x, 1, 1) - x)
        result += faces_ref[2, level] * (pltpu.roll(x, rows - 1, 0) - x)
        result += faces_ref[3, level] * (pltpu.roll(x, 1, 0) - x)
        work[level] = result

    def per_level(level, carry):
        one_pass(level, assemble(level, field_ref, edges))
        for sweep in range(PASSES - 1):
            one_pass(level, work[level])
        tile = work[level, 0:tile_rows, 0:tile_columns]
        smoothed[level] = tile
        if not last:
            for sweep in range(PASSES):
                one_pass(level, work[level])
            tile = work[level, 0:tile_rows, 0:tile_columns]
            start = pl.multiple_of(level * tile_rows, tile_rows)
            field_out[pl.ds(start, tile_rows), :] = sigma_ref[level] * tile
            return carry
        base, once = base_ref[level], once_ref[level]
        products = (base * base, base * once, once * once, once * tile)
        return tuple(c + jnp.sum(p, 0, keepdims=True) for c, p in zip(carry, products))

    sums = tuple(jnp.zeros((1, tile_columns), jnp.float32) for _ in range(4))
    sums = lax.fori_loop(0, levels, per_level, sums)
    if last:
        lane = lax.broadcasted_iota(jnp.int32, (1, tile_columns), 1)
        row = jnp.zeros((1, tile_columns), jnp.float32)
        for spot in range(4):
            row = jnp.where(lane == spot, jnp.sum(sums[spot], 1, keepdims=True), row)
        part[...] = row
        wait_for(arrived.at[pl.ds(0, devices - 1)], send)
        wait_for(back.at[pl.ds(0, devices - 1)], found_send)

        def tell(distance, carry):
            device = lax.rem(me + distance, devices)
            push(part, parts.at[distance - 1], part_send, part_receive, device)
            return carry

        lax.fori_loop(1, devices, tell, 0)
        wait_for(parts, part_receive)
        row = row + jnp.sum(parts[...], 0)
        s0, s1, s2, s3 = (
            jnp.sum(jnp.where(lane == spot, row, 0.0), 1, keepdims=True) for spot in range(4)
        )
        alpha = s0 / (s0 + s1)
        rest = s1 / (s0 + s1)
        norm = alpha * (alpha * s2 - rest * s1)
        along = rest + norm / s0
        norm_next = along * along * s0 - 2 * along * alpha * s1 + alpha * alpha * s2
        energy = along * along * s1 - 2 * along * alpha * s2 + alpha * alpha * s3
        step = norm / (norm_next + energy)
        scales = [
            alpha + step * along,
            step * alpha,
            rest - step * along,
            step * alpha - alpha - step * along,
        ]
        for spot in range(4):
            row = jnp.where(lane == spot, scales[spot], row)
        scale_out[...] = row
        wait_for(parts, part_send)
    else:
        wait_for(arrived.at[pl.ds(0, devices - 1)], send)
        if not first:
            wait_for(back.at[pl.ds(0, devices - 1)], found_send)


def phase(mode, number, place, obs_weights, weights, sigma, *more):
    first, last = mode == "first", mode == "last"
    held, width = obs_weights.shape[:2]
    devices = lax.axis_size("lat") * lax.axis_size("lon")
    levels, rows, columns = sigma.shape
    real = jnp.float32
    tile = jax.ShapeDtypeStruct(sigma.shape, real)
    flat = jax.ShapeDtypeStruct((levels * rows, columns), real)
    if first:
        outs = (tile, flat, jax.ShapeDtypeStruct((devices, 2, width), jnp.int32))
    elif last:
        outs = (tile, jax.ShapeDtypeStruct((1, columns), real))
    else:
        outs = (tile, flat)
    parcel = pltpu.VMEM((devices, 4 if first else 2, width), real)
    dma = pltpu.SemaphoreType.DMA
    scratch = [
        pltpu.VMEM(obs_weights.shape, real),
        pltpu.VMEM((width, held), real),
        pltpu.VMEM((held, width), real),
        parcel,
        parcel,
        pltpu.VMEM((512, 256), real),
        pltpu.VMEM(sigma.shape, real),
        pltpu.VMEM((levels, EDGE, rows), real),
        pltpu.VMEM((levels, EDGE, rows), real),
        pltpu.VMEM(weights.shape[1:], real),
        dma,
        dma,
        dma((devices * 2 // GROUP,)),
    ] + edge_scratch(levels, columns)
    if not first:
        scratch += [pltpu.VMEM((512, 256), jnp.bfloat16), parcel, parcel, dma, dma]
    if last:
        scratch += [
            pltpu.VMEM((1, columns), real),
            pltpu.VMEM((devices - 1, 1, columns), real),
            dma,
            dma,
        ]
    inputs = (place, obs_weights, weights, sigma) + more
    specs = [VMEM] * len(inputs)
    specs[1] = pl.BlockSpec(memory_space=pl.ANY)
    return pl.pallas_call(
        functools.partial(phase_kernel, mode),
        out_shape=outs,
        in_specs=specs,
        out_specs=(VMEM,) * len(outs),
        scratch_shapes=scratch,
        compiler_params=remote(number),
        name=mode,
    )(*inputs)


def body(sigma, east_coef, north_coef, mask, innovations, cells, owner, obs_weights):
    held = cells.shape[0]
    target = owner[:, 0]
    order = jnp.arange(held, dtype=jnp.int32)
    before = (target[:, None] == target[None, :]) & (order[:, None] < order[None, :])
    rank = jnp.sum(before.astype(jnp.int32), axis=0)
    place = jnp.stack([target * 2 + rank] * 8)
    stacked = jnp.concatenate([mask.astype(jnp.float32), east_coef, north_coef])
    weights = faces(stacked)
    fixed = (place, obs_weights, weights, sigma)
    base, base_field, here = phase("first", 1, *fixed, cells, innovations)
    once, once_field = phase("middle", 2, *fixed, here, base_field)
    again, scale = phase("last", 3, *fixed, here, once_field, base, once)
    scale = scale[0]
    increment = (scale[0] * base_field - scale[1] * once_field).reshape(sigma.shape)
    residual = scale[2] * base + scale[3] * once + scale[1] * again
    return (increment, residual)


def solution(mesh):
    return jax.shard_map(
        body,
        mesh=mesh,
        in_specs=(
            P(None, "lat", "lon"),
            P(None, "lat", "lon"),
            P(None, "lat", "lon"),
            P(None, "lat", "lon"),
            P(("lat", "lon"), None),
            P(("lat", "lon"), None),
            P(("lat", "lon"), None),
            P(("lat", "lon"), None, None),
        ),
        out_specs=(P(None, "lat", "lon"), P(None, "lat", "lon")),
        check_vma=False,
    )
```

```python
import functools

import jax
import jax.numpy as jnp
from jax import lax
from jax.experimental import pallas as pl
from jax.experimental.pallas import tpu as pltpu
from jax.sharding import PartitionSpec as P

PASSES = 5
EDGE = 16
GROUP = 16
STEP = 16
MESH = pl.DeviceIdType.MESH
EXACT = lax.Precision.HIGHEST
VMEM = pl.BlockSpec(memory_space=pltpu.VMEM)


def split(value):
    high = value.astype(jnp.bfloat16)
    low = (value - high.astype(jnp.float32)).astype(jnp.bfloat16)
    return high, low


def places(cells):
    line = cells >> 7
    numbers = line & 255, ((line >> 8) << 7) + (cells & 127)
    return numbers


def hits(numbers, width):
    lines = lax.broadcasted_iota(jnp.int32, (256, width), 0)
    return lines == numbers


def narrow_hits(numbers, width):
    lines = lax.broadcasted_iota(jnp.int32, (256, width), 0)
    narrow = [n.astype(jnp.float32).astype(jnp.bfloat16) for n in (lines, numbers)]
    return narrow[0] == narrow[1]


def neighbours():
    lats, lons = lax.axis_size("lat"), lax.axis_size("lon")
    lat, lon = lax.axis_index("lat"), lax.axis_index("lon")
    steps = [(1, 0), (-1, 0), (0, 1), (0, -1), (1, 1), (1, -1), (-1, 1), (-1, -1)]
    return [(lax.rem(lat + a + lats, lats), lax.rem(lon + b + lons, lons)) for a, b in steps]


def swap_edges(field_ref, low_ref, high_ref, edges, send, receive):
    partners = neighbours()
    rows = field_ref.shape[1]
    top = field_ref.at[:, rows - EDGE : rows, :]
    bottom = field_ref.at[:, 0:EDGE, :]
    sources = [top, bottom, high_ref, low_ref, top, top, bottom, bottom]
    landing = [1, 0, 3, 2, 7, 6, 5, 4]
    copies = []
    for number in (0, 1, 4, 5, 6, 7, 2, 3):
        partner = partners[number]
        copy = pltpu.make_async_remote_copy(
            src_ref=sources[number],
            dst_ref=edges.at[landing[number]],
            send_sem=send.at[number],
            recv_sem=receive.at[landing[number]],
            device_id=partner,
            device_id_type=MESH,
        )
        copy.start()
        copies.append(copy)
    return copies


def assemble(level, field_ref, edges):
    shape = (EDGE, field_ref.shape[2])
    lane = lax.broadcasted_iota(jnp.int32, shape, 1)

    def corner(east, west):
        inner = jnp.where(lane >= shape[1] - EDGE, edges[west, level], 0.0)
        return jnp.where(lane < EDGE, edges[east, level], inner)

    gap = jnp.zeros((shape[1] - 2 * EDGE, field_ref.shape[1]), jnp.float32)
    beside = jnp.concatenate([edges[2, level], gap, edges[3, level]], 0).T
    upper = jnp.concatenate([field_ref[level], beside], 1)
    north = jnp.concatenate([edges[0, level], corner(4, 5)], 1)
    south = jnp.concatenate([edges[1, level], corner(6, 7)], 1)
    return jnp.concatenate([upper, north, south], 0)


def build_faces(stacked_ref, edges, out_ref):
    levels = out_ref.shape[1]
    rows, columns = out_ref.shape[2:]
    tile_rows = stacked_ref.shape[1]
    line = lax.broadcasted_iota(jnp.int32, (rows, columns), 0)
    line = jnp.where(line < tile_rows + EDGE, line, line - tile_rows - 2 * EDGE)
    line = lax.axis_index("lat") * tile_rows + line
    inside = (line >= 0) & (line < tile_rows * lax.axis_size("lat"))

    def per_level(level, carry):
        land = jnp.where(inside, assemble(level, stacked_ref, edges), 0.0)
        east = assemble(levels + level, stacked_ref, edges)
        north = assemble(2 * levels + level, stacked_ref, edges)
        east = east * land * pltpu.roll(land, columns - 1, 1)
        north = north * land * pltpu.roll(land, rows - 1, 0)
        out_ref[0, level] = east
        out_ref[1, level] = pltpu.roll(east, 1, 1)
        out_ref[2, level] = north
        out_ref[3, level] = pltpu.roll(north, 1, 0)
        return carry

    lax.fori_loop(0, levels, per_level, 0)


def edge_scratch(levels, columns):
    return [
        pltpu.VMEM((8, levels, EDGE, columns), jnp.float32),
        pltpu.SemaphoreType.DMA((8,)),
        pltpu.SemaphoreType.DMA((8,)),
    ]


def remote(number):
    return pltpu.CompilerParams(
        vmem_limit_bytes=48 * 1024 * 1024, collective_id=number, has_side_effects=True
    )


def everyone():
    lats, lons = lax.axis_size("lat"), lax.axis_size("lon")
    return lats * lons, lax.axis_index("lat") * lons + lax.axis_index("lon")


def where_is(device):
    lons = lax.axis_size("lon")
    return lax.div(device, lons), lax.rem(device, lons)


def greet_everyone():
    devices, me = everyone()
    barrier = pltpu.get_barrier_semaphore()

    def greet(distance, carry):
        partner = where_is(lax.rem(me + distance, devices))
        pl.semaphore_signal(barrier, inc=1, device_id=partner, device_id_type=MESH)
        return carry

    lax.fori_loop(1, devices, greet, 0)
    pl.semaphore_wait(barrier, devices - 1)


def push(source, target, send, receive, device):
    pltpu.make_async_remote_copy(
        src_ref=source,
        dst_ref=target,
        send_sem=send,
        recv_sem=receive,
        device_id=where_is(device),
        device_id_type=MESH,
    ).start()


def wait_for(ref, semaphore):
    pltpu.make_async_copy(ref, ref, semaphore).wait()


def gather_and_send(here, field_ref, turned, found_ref, back, send, receive):
    square = jnp.concatenate([field_ref[0:256], field_ref[256:512]], 1).T
    high, low = split(square)
    turned[0:256] = high
    turned[256:512] = low
    devices, me = everyone()
    ranks, width = here.shape[1:]
    batch = GROUP // ranks
    groups = devices // batch
    zero, one = jnp.bfloat16(0), jnp.bfloat16(1)

    def group_of(turn):
        return lax.rem(lax.div(me, batch) + turn, groups)

    def send_group(turn):
        for item in range(batch):
            device = group_of(turn) * batch + item

            @pl.when(device != me)
            def _():
                push(found_ref.at[device], back.at[me], send, receive, device)

            @pl.when(device == me)
            def _():
                pltpu.make_async_copy(found_ref.at[device], back.at[device], receive).start()

    def step(turn, carry):
        start = group_of(turn) * batch
        places_of = [
            places(here[start + item // ranks, item % ranks : item % ranks + 1])
            for item in range(GROUP)
        ]
        right = [
            jnp.where(narrow_hits(row, width), one, zero) for row, _ in places_of
        ]
        found = jnp.dot(
            turned[...], jnp.concatenate(right, 1), preferred_element_type=jnp.float32
        )
        found = found[0:256] + found[256:512]
        for item in range(GROUP):
            part = found[:, item * width : (item + 1) * width]
            part = jnp.where(hits(places_of[item][1], width), part, 0.0)
            spot = item % ranks
            found_ref[start + item // ranks, spot : spot + 1] = jnp.sum(part, 0, keepdims=True)

        @pl.when(turn > 0)
        def _():
            send_group(turn - 1)

        return carry

    lax.fori_loop(0, groups, step, 0)
    send_group(groups - 1)
    wait_for(back, receive)


def weigh(turned, weights_ref, weighted):
    held = turned.shape[1]

    def step(number, carry):
        values = turned[...]
        start = pl.multiple_of(number * STEP, STEP)
        rows = []
        for item in range(STEP):
            column = values[:, item : item + 1]
            rows.append(jnp.sum(weights_ref[start + item] * column, 0, keepdims=True))
        weighted[pl.ds(start, STEP), :] = jnp.concatenate(rows, 0)
        turned[...] = pltpu.roll(values, held - STEP, 1)
        return carry

    lax.fori_loop(0, held // STEP, step, 0)


def scatter_arrivals(first, here, parcel, arrived, total, send, receive, between):
    devices, me = everyone()
    ranks, width = here.shape[1:]
    batch = GROUP // ranks
    groups = devices // batch
    mine = lax.div(me, batch)
    zero, one = jnp.bfloat16(0), jnp.bfloat16(1)

    pltpu.make_async_copy(parcel.at[me], arrived.at[me], receive.at[mine]).start()

    def tell(distance, carry):
        device = lax.rem(me + distance, devices)
        push(parcel.at[device], arrived.at[me], send, receive.at[mine], device)
        return carry

    lax.fori_loop(1, devices, tell, 0)
    between()

    def step(turn, carry):
        group = lax.rem(mine + 2 * groups - 1 - turn, groups)
        start = group * batch
        wait_for(arrived.at[pl.ds(start, batch)], receive.at[group])
        left, right = [], []
        for item in range(GROUP):
            device, spot = start + item // ranks, item % ranks
            if first:
                cells = arrived[device, spot : spot + 1].astype(jnp.int32)
                here[device, spot : spot + 1] = cells
                value = arrived[device, ranks + spot : ranks + spot + 1]
            else:
                cells = here[device, spot : spot + 1]
                value = arrived[device, spot : spot + 1]
            row, column = places(cells)
            row_hit = narrow_hits(row, width)
            left.append(jnp.concatenate([jnp.where(row_hit, part, zero) for part in split(value)], 0))
            right.append(jnp.where(narrow_hits(column, width), one, zero))
        total[...] += lax.dot_general(
            jnp.concatenate(left, 1),
            jnp.concatenate(right, 1),
            (((1,), (1,)), ((), ())),
            preferred_element_type=jnp.float32,
        )
        return carry

    lax.fori_loop(0, groups, step, 0)


def phase_kernel(mode, *refs):
    first, last = mode == "first", mode == "last"
    place_ref, weights_hbm, sigma_ref = refs[:3]
    refs = refs[3:]
    if first:
        cells_ref, value_ref, stacked_ref, stacked_low, stacked_high = refs[:5]
        smoothed, field_out, here, faces_ref = refs[5:9]
        refs = refs[9:]
    elif last:
        faces_ref, here, seen_ref, base_ref, once_ref, base_seen_ref = refs[:6]
        smoothed, increment = refs[6:8]
        refs = refs[8:]
    else:
        faces_ref, here, seen_ref, smoothed, field_out = refs[:5]
        refs = refs[5:]
    weights_ref, turned, weighted, parcel, arrived, total, field_ref, low, high, work = refs[:10]
    copied, send, receive, edges, edge_send, edge_receive = refs[10:16]
    refs = refs[16:]
    if first:
        stacked_edges, stacked_send, stacked_receive = refs
    else:
        square, found, back, found_send, found_receive = refs[:5]
        refs = refs[5:]
    if last:
        part, parts, part_send, part_receive = refs

    load = pltpu.make_async_copy(weights_hbm, weights_ref, copied)
    load.start()
    greet_everyone()
    devices, me = everyone()
    ranks, width = here.shape[1:]
    held = turned.shape[1]
    number = lax.broadcasted_iota(jnp.int32, (devices, held), 0)

    def placing(rank):
        return jnp.where(number * ranks + rank == place_ref[0:1], 1.0, 0.0)

    stacked_copies = []
    if first:
        stacked_copies = swap_edges(
            stacked_ref, stacked_low, stacked_high, stacked_edges, stacked_send, stacked_receive
        )
        turned[...] = value_ref[...].T
    else:
        gather_and_send(here, seen_ref, square, found, back, found_send, found_receive)
        turned[...] = sum(
            lax.dot_general(
                back[:, rank, :],
                placing(rank),
                (((0,), (0,)), ((), ())),
                precision=EXACT,
                preferred_element_type=jnp.float32,
            )
            for rank in range(ranks)
        )
    load.wait()
    weigh(turned, weights_ref, weighted)
    for rank in range(ranks):
        chosen = placing(rank)
        if first:
            parcel[:, rank, :] = jnp.dot(
                chosen,
                cells_ref[...].astype(jnp.float32),
                precision=EXACT,
                preferred_element_type=jnp.float32,
            )
        parcel[:, (ranks if first else 0) + rank, :] = jnp.dot(
            chosen, weighted[...], precision=EXACT, preferred_element_type=jnp.float32
        )
    total[...] = jnp.zeros_like(total)

    def between():
        if first:
            for copy in stacked_copies:
                copy.wait()
            build_faces(stacked_ref, stacked_edges, faces_ref)

    scatter_arrivals(first, here, parcel, arrived, total, send, receive, between)

    field = total[0:256] + total[256:512]
    levels, tile_rows, tile_columns = field_ref.shape
    for level in range(levels):
        start, side = level * 128 % 256, level * 128 // 256 * 128
        tile = field[start : start + 128, side : side + 128] * sigma_ref[level]
        field_ref[level] = tile
        flat = tile.T
        low[level] = flat[0:EDGE]
        high[level] = flat[tile_columns - EDGE :]
    copies = swap_edges(field_ref, low, high, edges, edge_send, edge_receive)
    for copy in copies:
        copy.wait()
    rows, columns = work.shape[1:]

    def one_pass(level, x):
        result = x + faces_ref[0, level] * (pltpu.roll(x, columns - 1, 1) - x)
        result += faces_ref[1, level] * (pltpu.roll(x, 1, 1) - x)
        result += faces_ref[2, level] * (pltpu.roll(x, rows - 1, 0) - x)
        result += faces_ref[3, level] * (pltpu.roll(x, 1, 0) - x)
        work[level] = result

    def per_level(level, carry):
        one_pass(level, assemble(level, field_ref, edges))
        for sweep in range(PASSES - 1):
            one_pass(level, work[level])
        tile = work[level, 0:tile_rows, 0:tile_columns]
        smoothed[level] = tile
        if not last:
            for sweep in range(PASSES):
                one_pass(level, work[level])
            tile = work[level, 0:tile_rows, 0:tile_columns]
            start = pl.multiple_of(level * tile_rows, tile_rows)
            field_out[pl.ds(start, tile_rows), :] = sigma_ref[level] * tile
            return carry
        base, once = base_ref[level], once_ref[level]
        products = (base * base, base * once, once * once, once * tile)
        return tuple(c + jnp.sum(p, 0, keepdims=True) for c, p in zip(carry, products))

    sums = tuple(jnp.zeros((1, tile_columns), jnp.float32) for _ in range(4))
    sums = lax.fori_loop(0, levels, per_level, sums)
    if last:
        lane = lax.broadcasted_iota(jnp.int32, (1, tile_columns), 1)
        row = jnp.zeros((1, tile_columns), jnp.float32)
        for spot in range(4):
            row = jnp.where(lane == spot, jnp.sum(sums[spot], 1, keepdims=True), row)
        part[...] = row
        wait_for(arrived.at[pl.ds(0, devices - 1)], send)
        wait_for(back.at[pl.ds(0, devices - 1)], found_send)

        def tell(distance, carry):
            device = lax.rem(me + distance, devices)
            push(part, parts.at[distance - 1], part_send, part_receive, device)
            return carry

        lax.fori_loop(1, devices, tell, 0)
        wait_for(parts, part_receive)
        row = row + jnp.sum(parts[...], 0)
        s0, s1, s2, s3 = (
            jnp.sum(jnp.where(lane == spot, row, 0.0), 1, keepdims=True) for spot in range(4)
        )
        alpha = s0 / (s0 + s1)
        rest = s1 / (s0 + s1)
        norm = alpha * (alpha * s2 - rest * s1)
        along = rest + norm / s0
        norm_next = along * along * s0 - 2 * along * alpha * s1 + alpha * alpha * s2
        energy = along * along * s1 - 2 * along * alpha * s2 + alpha * alpha * s3
        step = norm / (norm_next + energy)
        scales = [
            alpha + step * along,
            step * alpha,
            rest - step * along,
            step * alpha - alpha - step * along,
        ]
        for level in range(levels):
            flat = slice(level * tile_rows, (level + 1) * tile_rows)
            increment[level] = scales[0] * base_seen_ref[flat] - scales[1] * seen_ref[flat]
            smoothed[level] = (
                scales[2] * base_ref[level]
                + scales[3] * once_ref[level]
                + scales[1] * smoothed[level]
            )
        wait_for(parts, part_send)
    else:
        wait_for(arrived.at[pl.ds(0, devices - 1)], send)
        if not first:
            wait_for(back.at[pl.ds(0, devices - 1)], found_send)


def phase(mode, number, place, obs_weights, sigma, *more):
    first, last = mode == "first", mode == "last"
    held, width = obs_weights.shape[:2]
    devices = lax.axis_size("lat") * lax.axis_size("lon")
    levels, rows, columns = sigma.shape
    real = jnp.float32
    padded = (levels, rows + 2 * EDGE, 2 * columns)
    tile = jax.ShapeDtypeStruct(sigma.shape, real)
    flat = jax.ShapeDtypeStruct((levels * rows, columns), real)
    if first:
        outs = (tile, flat, jax.ShapeDtypeStruct((devices, 2, width), jnp.int32))
        outs += (jax.ShapeDtypeStruct((4,) + padded, real),)
    elif last:
        outs = (tile, tile)
    else:
        outs = (tile, flat)
    parcel = pltpu.VMEM((devices, 4 if first else 2, width), real)
    dma = pltpu.SemaphoreType.DMA
    scratch = [
        pltpu.VMEM(obs_weights.shape, real),
        pltpu.VMEM((width, held), real),
        pltpu.VMEM((held, width), real),
        parcel,
        parcel,
        pltpu.VMEM((512, 256), real),
        pltpu.VMEM(sigma.shape, real),
        pltpu.VMEM((levels, EDGE, rows), real),
        pltpu.VMEM((levels, EDGE, rows), real),
        pltpu.VMEM(padded, real),
        dma,
        dma,
        dma((devices * 2 // GROUP,)),
    ] + edge_scratch(levels, columns)
    if first:
        scratch += edge_scratch(3 * levels, columns)
    else:
        scratch += [pltpu.VMEM((512, 256), jnp.bfloat16), parcel, parcel, dma, dma]
    if last:
        scratch += [
            pltpu.VMEM((1, columns), real),
            pltpu.VMEM((devices - 1, 1, columns), real),
            dma,
            dma,
        ]
    inputs = (place, obs_weights, sigma) + more
    specs = [VMEM] * len(inputs)
    specs[1] = pl.BlockSpec(memory_space=pl.ANY)
    return pl.pallas_call(
        functools.partial(phase_kernel, mode),
        out_shape=outs,
        in_specs=specs,
        out_specs=(VMEM,) * len(outs),
        scratch_shapes=scratch,
        compiler_params=remote(number),
        name=mode,
    )(*inputs)


def body(sigma, east_coef, north_coef, mask, innovations, cells, owner, obs_weights):
    held = cells.shape[0]
    target = owner[:, 0]
    order = jnp.arange(held, dtype=jnp.int32)
    before = (target[:, None] == target[None, :]) & (order[:, None] < order[None, :])
    rank = jnp.sum(before.astype(jnp.int32), axis=0)
    place = jnp.stack([target * 2 + rank] * 8)
    stacked = jnp.concatenate([mask.astype(jnp.float32), east_coef, north_coef])
    columns = stacked.shape[2]
    low = jnp.swapaxes(stacked[:, :, :EDGE], 1, 2)
    high = jnp.swapaxes(stacked[:, :, columns - EDGE :], 1, 2)
    fixed = (place, obs_weights, sigma)
    base, base_field, here, weights = phase(
        "first", 1, *fixed, cells, innovations, stacked, low, high
    )
    once, once_field = phase("middle", 2, *fixed, weights, here, base_field)
    residual, increment = phase(
        "last", 3, *fixed, weights, here, once_field, base, once, base_field
    )
    return (increment, residual)


def solution(mesh):
    return jax.shard_map(
        body,
        mesh=mesh,
        in_specs=(
            P(None, "lat", "lon"),
            P(None, "lat", "lon"),
            P(None, "lat", "lon"),
            P(None, "lat", "lon"),
            P(("lat", "lon"), None),
            P(("lat", "lon"), None),
            P(("lat", "lon"), None),
            P(("lat", "lon"), None, None),
        ),
        out_specs=(P(None, "lat", "lon"), P(None, "lat", "lon")),
        check_vma=False,
    )
```

```python
import functools

import jax
import jax.numpy as jnp
from jax import lax
from jax.experimental import pallas as pl
from jax.experimental.pallas import tpu as pltpu
from jax.sharding import PartitionSpec as P

PASSES = 5
EDGE = 16
GROUP = 16
STEP = 16
MESH = pl.DeviceIdType.MESH
EXACT = lax.Precision.HIGHEST
VMEM = pl.BlockSpec(memory_space=pltpu.VMEM)


def split(value):
    high = value.astype(jnp.bfloat16)
    low = (value - high.astype(jnp.float32)).astype(jnp.bfloat16)
    return high, low


def places(cells):
    line = cells >> 7
    numbers = line & 255, ((line >> 8) << 7) + (cells & 127)
    return numbers


def hits(numbers, width):
    lines = lax.broadcasted_iota(jnp.int32, (256, width), 0)
    return lines == numbers


def narrow_hits(numbers, width):
    lines = lax.broadcasted_iota(jnp.int32, (256, width), 0)
    narrow = [n.astype(jnp.float32).astype(jnp.bfloat16) for n in (lines, numbers)]
    return narrow[0] == narrow[1]


def neighbours():
    lats, lons = lax.axis_size("lat"), lax.axis_size("lon")
    lat, lon = lax.axis_index("lat"), lax.axis_index("lon")
    steps = [(1, 0), (-1, 0), (0, 1), (0, -1), (1, 1), (1, -1), (-1, 1), (-1, -1)]
    return [(lax.rem(lat + a + lats, lats), lax.rem(lon + b + lons, lons)) for a, b in steps]


def swap_edges(field_ref, low_ref, high_ref, edges, send, receive):
    partners = neighbours()
    rows = field_ref.shape[1]
    top = field_ref.at[:, rows - EDGE : rows, :]
    bottom = field_ref.at[:, 0:EDGE, :]
    sources = [top, bottom, high_ref, low_ref, top, top, bottom, bottom]
    landing = [1, 0, 3, 2, 7, 6, 5, 4]
    copies = []
    for number in (0, 1, 4, 5, 6, 7, 2, 3):
        partner = partners[number]
        copy = pltpu.make_async_remote_copy(
            src_ref=sources[number],
            dst_ref=edges.at[landing[number]],
            send_sem=send.at[number],
            recv_sem=receive.at[landing[number]],
            device_id=partner,
            device_id_type=MESH,
        )
        copy.start()
        copies.append(copy)
    return copies


def assemble(level, field_ref, edges):
    shape = (EDGE, field_ref.shape[2])
    lane = lax.broadcasted_iota(jnp.int32, shape, 1)

    def corner(east, west):
        inner = jnp.where(lane >= shape[1] - EDGE, edges[west, level], 0.0)
        return jnp.where(lane < EDGE, edges[east, level], inner)

    gap = jnp.zeros((shape[1] - 2 * EDGE, field_ref.shape[1]), jnp.float32)
    beside = jnp.concatenate([edges[2, level], gap, edges[3, level]], 0).T
    upper = jnp.concatenate([field_ref[level], beside], 1)
    north = jnp.concatenate([edges[0, level], corner(4, 5)], 1)
    south = jnp.concatenate([edges[1, level], corner(6, 7)], 1)
    return jnp.concatenate([upper, north, south], 0)


def build_faces(stacked_ref, edges, out_ref):
    levels = out_ref.shape[1]
    rows, columns = out_ref.shape[2:]
    tile_rows = stacked_ref.shape[1]
    line = lax.broadcasted_iota(jnp.int32, (rows, columns), 0)
    line = jnp.where(line < tile_rows + EDGE, line, line - tile_rows - 2 * EDGE)
    line = lax.axis_index("lat") * tile_rows + line
    inside = (line >= 0) & (line < tile_rows * lax.axis_size("lat"))

    def per_level(level, carry):
        land = jnp.where(inside, assemble(level, stacked_ref, edges), 0.0)
        east = assemble(levels + level, stacked_ref, edges)
        north = assemble(2 * levels + level, stacked_ref, edges)
        east = east * land * pltpu.roll(land, columns - 1, 1)
        north = north * land * pltpu.roll(land, rows - 1, 0)
        out_ref[0, level] = east
        out_ref[1, level] = pltpu.roll(east, 1, 1)
        out_ref[2, level] = north
        out_ref[3, level] = pltpu.roll(north, 1, 0)
        return carry

    lax.fori_loop(0, levels, per_level, 0)


def edge_scratch(levels, columns):
    return [
        pltpu.VMEM((8, levels, EDGE, columns), jnp.float32),
        pltpu.SemaphoreType.DMA((8,)),
        pltpu.SemaphoreType.DMA((8,)),
    ]


def remote(number):
    return pltpu.CompilerParams(
        vmem_limit_bytes=48 * 1024 * 1024, collective_id=number, has_side_effects=True
    )


def everyone():
    lats, lons = lax.axis_size("lat"), lax.axis_size("lon")
    return lats * lons, lax.axis_index("lat") * lons + lax.axis_index("lon")


def where_is(device):
    lons = lax.axis_size("lon")
    return lax.div(device, lons), lax.rem(device, lons)


def greet_everyone():
    devices, me = everyone()
    barrier = pltpu.get_barrier_semaphore()

    def greet(distance, carry):
        partner = where_is(lax.rem(me + distance, devices))
        pl.semaphore_signal(barrier, inc=1, device_id=partner, device_id_type=MESH)
        return carry

    lax.fori_loop(1, devices, greet, 0)
    return barrier


def push(source, target, send, receive, device):
    pltpu.make_async_remote_copy(
        src_ref=source,
        dst_ref=target,
        send_sem=send,
        recv_sem=receive,
        device_id=where_is(device),
        device_id_type=MESH,
    ).start()


def wait_for(ref, semaphore):
    pltpu.make_async_copy(ref, ref, semaphore).wait()


def gather_and_send(here, field_ref, turned, found_ref, back, send, receive):
    square = jnp.concatenate([field_ref[0:256], field_ref[256:512]], 1).T
    high, low = split(square)
    turned[0:256] = high
    turned[256:512] = low
    devices, me = everyone()
    ranks, width = here.shape[1:]
    batch = GROUP // ranks
    groups = devices // batch
    zero, one = jnp.bfloat16(0), jnp.bfloat16(1)

    def group_of(turn):
        return lax.rem(lax.div(me, batch) + turn, groups)

    def send_group(turn):
        for item in range(batch):
            device = group_of(turn) * batch + item

            @pl.when(device != me)
            def _():
                push(found_ref.at[device], back.at[me], send, receive, device)

            @pl.when(device == me)
            def _():
                pltpu.make_async_copy(found_ref.at[device], back.at[device], receive).start()

    def step(turn, carry):
        start = group_of(turn) * batch
        places_of = [
            places(here[start + item // ranks, item % ranks : item % ranks + 1])
            for item in range(GROUP)
        ]
        right = [
            jnp.where(narrow_hits(row, width), one, zero) for row, _ in places_of
        ]
        found = jnp.dot(
            turned[...], jnp.concatenate(right, 1), preferred_element_type=jnp.float32
        )
        found = found[0:256] + found[256:512]
        for item in range(GROUP):
            part = found[:, item * width : (item + 1) * width]
            part = jnp.where(hits(places_of[item][1], width), part, 0.0)
            spot = item % ranks
            found_ref[start + item // ranks, spot : spot + 1] = jnp.sum(part, 0, keepdims=True)

        @pl.when(turn > 0)
        def _():
            send_group(turn - 1)

        return carry

    lax.fori_loop(0, groups, step, 0)
    send_group(groups - 1)
    wait_for(back, receive)


def weigh(turned, weights_ref, weighted):
    held = turned.shape[1]

    def step(number, carry):
        values = turned[...]
        start = pl.multiple_of(number * STEP, STEP)
        rows = []
        for item in range(STEP):
            column = values[:, item : item + 1]
            rows.append(jnp.sum(weights_ref[start + item] * column, 0, keepdims=True))
        weighted[pl.ds(start, STEP), :] = jnp.concatenate(rows, 0)
        turned[...] = pltpu.roll(values, held - STEP, 1)
        return carry

    lax.fori_loop(0, held // STEP, step, 0)


def scatter_arrivals(first, here, parcel, arrived, total, send, receive, between):
    devices, me = everyone()
    ranks, width = here.shape[1:]
    batch = GROUP // ranks
    groups = devices // batch
    mine = lax.div(me, batch)
    zero, one = jnp.bfloat16(0), jnp.bfloat16(1)

    pltpu.make_async_copy(parcel.at[me], arrived.at[me], receive.at[mine]).start()

    def tell(distance, carry):
        device = lax.rem(me + distance, devices)
        push(parcel.at[device], arrived.at[me], send, receive.at[mine], device)
        return carry

    lax.fori_loop(1, devices, tell, 0)
    between()

    def step(turn, carry):
        group = lax.rem(mine + 2 * groups - 1 - turn, groups)
        start = group * batch
        wait_for(arrived.at[pl.ds(start, batch)], receive.at[group])
        left, right = [], []
        for item in range(GROUP):
            device, spot = start + item // ranks, item % ranks
            if first:
                cells = arrived[device, spot : spot + 1].astype(jnp.int32)
                here[device, spot : spot + 1] = cells
                value = arrived[device, ranks + spot : ranks + spot + 1]
            else:
                cells = here[device, spot : spot + 1]
                value = arrived[device, spot : spot + 1]
            row, column = places(cells)
            row_hit = narrow_hits(row, width)
            left.append(jnp.concatenate([jnp.where(row_hit, part, zero) for part in split(value)], 0))
            right.append(jnp.where(narrow_hits(column, width), one, zero))
        total[...] += lax.dot_general(
            jnp.concatenate(left, 1),
            jnp.concatenate(right, 1),
            (((1,), (1,)), ((), ())),
            preferred_element_type=jnp.float32,
        )
        return carry

    lax.fori_loop(0, groups, step, 0)


def phase(mode, place_ref, weights_ref, sigma_ref, faces_ref, here, common, sparse, more):
    first, last = mode == "first", mode == "last"
    turned, weighted, total, field_ref, low, high, work = common[:7]
    send, receive, edges, edge_send, edge_receive = common[7:12]
    parcel, arrived = sparse[:2]
    if first:
        cells_ref, value_ref, ready, smoothed, field_out, stacked = more
    else:
        square, found, back, found_send, found_receive = sparse[2:]
    if last:
        seen_ref, base_ref, once_ref, base_seen_ref, smoothed, increment = more[:6]
        part, parts, part_send, part_receive = more[6:]
    elif not first:
        seen_ref, smoothed, field_out = more
    devices, me = everyone()
    ranks, width = here.shape[1:]
    held = turned.shape[1]
    number = lax.broadcasted_iota(jnp.int32, (devices, held), 0)

    def placing(rank):
        return jnp.where(number * ranks + rank == place_ref[0:1], 1.0, 0.0)

    stacked_copies = []
    if first:
        stacked_copies = swap_edges(*stacked)
        turned[...] = value_ref[...].T
    else:
        gather_and_send(here, seen_ref, square, found, back, found_send, found_receive)
        turned[...] = sum(
            lax.dot_general(
                back[:, rank, :],
                placing(rank),
                (((0,), (0,)), ((), ())),
                precision=EXACT,
                preferred_element_type=jnp.float32,
            )
            for rank in range(ranks)
        )
    if first:
        ready()
    weigh(turned, weights_ref, weighted)
    for rank in range(ranks):
        chosen = placing(rank)
        if first:
            parcel[:, rank, :] = jnp.dot(
                chosen,
                cells_ref[...].astype(jnp.float32),
                precision=EXACT,
                preferred_element_type=jnp.float32,
            )
        parcel[:, (ranks if first else 0) + rank, :] = jnp.dot(
            chosen, weighted[...], precision=EXACT, preferred_element_type=jnp.float32
        )
    total[...] = jnp.zeros_like(total)

    def between():
        if first:
            for copy in stacked_copies:
                copy.wait()
            build_faces(stacked[0], stacked[3], faces_ref)

    scatter_arrivals(first, here, parcel, arrived, total, send, receive, between)

    field = total[0:256] + total[256:512]
    levels, tile_rows, tile_columns = field_ref.shape
    for level in range(levels):
        start, side = level * 128 % 256, level * 128 // 256 * 128
        tile = field[start : start + 128, side : side + 128] * sigma_ref[level]
        field_ref[level] = tile
        flat = tile.T
        low[level] = flat[0:EDGE]
        high[level] = flat[tile_columns - EDGE :]
    copies = swap_edges(field_ref, low, high, edges, edge_send, edge_receive)
    for copy in copies:
        copy.wait()
    rows, columns = work.shape[1:]

    def one_pass(level, x):
        result = x + faces_ref[0, level] * (pltpu.roll(x, columns - 1, 1) - x)
        result += faces_ref[1, level] * (pltpu.roll(x, 1, 1) - x)
        result += faces_ref[2, level] * (pltpu.roll(x, rows - 1, 0) - x)
        result += faces_ref[3, level] * (pltpu.roll(x, 1, 0) - x)
        work[level] = result

    def per_level(level, carry):
        one_pass(level, assemble(level, field_ref, edges))
        for sweep in range(PASSES - 1):
            one_pass(level, work[level])
        tile = work[level, 0:tile_rows, 0:tile_columns]
        smoothed[level] = tile
        if not last:
            for sweep in range(PASSES):
                one_pass(level, work[level])
            tile = work[level, 0:tile_rows, 0:tile_columns]
            start = pl.multiple_of(level * tile_rows, tile_rows)
            field_out[pl.ds(start, tile_rows), :] = sigma_ref[level] * tile
            return carry
        base, once = base_ref[level], once_ref[level]
        products = (base * base, base * once, once * once, once * tile)
        return tuple(c + jnp.sum(p, 0, keepdims=True) for c, p in zip(carry, products))

    sums = tuple(jnp.zeros((1, tile_columns), jnp.float32) for _ in range(4))
    sums = lax.fori_loop(0, levels, per_level, sums)
    if last:
        lane = lax.broadcasted_iota(jnp.int32, (1, tile_columns), 1)
        row = jnp.zeros((1, tile_columns), jnp.float32)
        for spot in range(4):
            row = jnp.where(lane == spot, jnp.sum(sums[spot], 1, keepdims=True), row)
        part[...] = row
        wait_for(arrived.at[pl.ds(0, devices - 1)], send)
        wait_for(back.at[pl.ds(0, devices - 1)], found_send)

        def tell(distance, carry):
            device = lax.rem(me + distance, devices)
            push(part, parts.at[distance - 1], part_send, part_receive, device)
            return carry

        lax.fori_loop(1, devices, tell, 0)
        wait_for(parts, part_receive)
        row = row + jnp.sum(parts[...], 0)
        s0, s1, s2, s3 = (
            jnp.sum(jnp.where(lane == spot, row, 0.0), 1, keepdims=True) for spot in range(4)
        )
        alpha = s0 / (s0 + s1)
        rest = s1 / (s0 + s1)
        norm = alpha * (alpha * s2 - rest * s1)
        along = rest + norm / s0
        norm_next = along * along * s0 - 2 * along * alpha * s1 + alpha * alpha * s2
        energy = along * along * s1 - 2 * along * alpha * s2 + alpha * alpha * s3
        step = norm / (norm_next + energy)
        scales = [
            alpha + step * along,
            step * alpha,
            rest - step * along,
            step * alpha - alpha - step * along,
        ]
        for level in range(levels):
            flat = slice(level * tile_rows, (level + 1) * tile_rows)
            increment[level] = scales[0] * base_seen_ref[flat] - scales[1] * seen_ref[flat]
            smoothed[level] = (
                scales[2] * base_ref[level]
                + scales[3] * once_ref[level]
                + scales[1] * smoothed[level]
            )
        wait_for(parts, part_send)
    else:
        wait_for(arrived.at[pl.ds(0, devices - 1)], send)
        if not first:
            wait_for(back.at[pl.ds(0, devices - 1)], found_send)


def kernel(*refs):
    place_ref, weights_hbm, sigma_ref, cells_ref, value_ref, mask_ref, east_ref, north_ref = refs[:8]
    increment, residual = refs[8:10]
    base, once, base_field, once_field, here, faces_ref, weights_ref, copied = refs[10:18]
    common, wide, narrow = refs[18:30], refs[30:32], refs[32:39]
    stacked, finish = refs[39:45], refs[45:]
    load = pltpu.make_async_copy(weights_hbm, weights_ref, copied)
    load.start()
    barrier = greet_everyone()
    fields, low, high = stacked[:3]
    levels, rows, columns = sigma_ref.shape
    for kind, ref in enumerate((mask_ref, east_ref, north_ref)):
        for level in range(levels):
            tile = ref[level].astype(jnp.float32)
            flat = tile.T
            fields[kind * levels + level] = tile
            low[kind * levels + level] = flat[0:EDGE]
            high[kind * levels + level] = flat[columns - EDGE :]
    pl.semaphore_wait(barrier, everyone()[0] - 1)
    fixed = (place_ref, weights_ref, sigma_ref, faces_ref, here, common)
    phase("first", *fixed, wide, (cells_ref, value_ref, load.wait, base, base_field, stacked))
    phase("middle", *fixed, narrow, (base_field, once, once_field))
    phase(
        "last",
        *fixed,
        narrow,
        (once_field, base, once, base_field, residual, increment) + finish,
    )


def body(sigma, east_coef, north_coef, mask, innovations, cells, owner, obs_weights):
    held, width = cells.shape
    devices = lax.axis_size("lat") * lax.axis_size("lon")
    levels, rows, columns = sigma.shape
    target = owner[:, 0]
    order = jnp.arange(held, dtype=jnp.int32)
    before = (target[:, None] == target[None, :]) & (order[:, None] < order[None, :])
    rank = jnp.sum(before.astype(jnp.int32), axis=0)
    place = jnp.stack([target * 2 + rank] * 8)
    real = jnp.float32
    dma = pltpu.SemaphoreType.DMA
    padded = (levels, rows + 2 * EDGE, 2 * columns)
    tile = pltpu.VMEM(sigma.shape, real)
    flat = pltpu.VMEM((levels * rows, columns), real)
    parcel = pltpu.VMEM((devices, 2, width), real)
    twice = pltpu.VMEM((devices, 4, width), real)
    strip = pltpu.VMEM((levels, EDGE, rows), real)
    strips = pltpu.VMEM((3 * levels, EDGE, rows), real)
    scratch = [tile, tile, flat, flat, pltpu.VMEM((devices, 2, width), jnp.int32)]
    scratch += [pltpu.VMEM((4,) + padded, real), pltpu.VMEM(obs_weights.shape, real), dma]
    scratch += [
        pltpu.VMEM((width, held), real),
        pltpu.VMEM((held, width), real),
        pltpu.VMEM((512, 256), real),
        tile,
        strip,
        strip,
        pltpu.VMEM(padded, real),
        dma,
        dma((devices * 2 // GROUP,)),
    ] + edge_scratch(levels, columns)
    scratch += [twice, twice]
    scratch += [parcel, parcel, pltpu.VMEM((512, 256), jnp.bfloat16), parcel, parcel, dma, dma]
    scratch += [pltpu.VMEM((3 * levels, rows, columns), real), strips, strips]
    scratch += edge_scratch(3 * levels, columns)
    scratch += [
        pltpu.VMEM((1, columns), real),
        pltpu.VMEM((devices - 1, 1, columns), real),
        dma,
        dma,
    ]
    specs = [VMEM] * 8
    specs[1] = pl.BlockSpec(memory_space=pl.ANY)
    out = jax.ShapeDtypeStruct(sigma.shape, real)
    return pl.pallas_call(
        kernel,
        out_shape=(out, out),
        in_specs=specs,
        out_specs=(VMEM, VMEM),
        scratch_shapes=scratch,
        compiler_params=remote(1),
        name="whole",
    )(place, obs_weights, sigma, cells, innovations, mask, east_coef, north_coef)


def solution(mesh):
    return jax.shard_map(
        body,
        mesh=mesh,
        in_specs=(
            P(None, "lat", "lon"),
            P(None, "lat", "lon"),
            P(None, "lat", "lon"),
            P(None, "lat", "lon"),
            P(("lat", "lon"), None),
            P(("lat", "lon"), None),
            P(("lat", "lon"), None),
            P(("lat", "lon"), None, None),
        ),
        out_specs=(P(None, "lat", "lon"), P(None, "lat", "lon")),
        check_vma=False,
    )
```

```python
import functools

import jax
import jax.numpy as jnp
from jax import lax
from jax.experimental import pallas as pl
from jax.experimental.pallas import tpu as pltpu
from jax.sharding import PartitionSpec as P

PASSES = 5
EDGE = 16
GROUP = 32
STEP = 16
MESH = pl.DeviceIdType.MESH
EXACT = lax.Precision.HIGHEST
VMEM = pl.BlockSpec(memory_space=pltpu.VMEM)


def split(value):
    high = value.astype(jnp.bfloat16)
    low = (value - high.astype(jnp.float32)).astype(jnp.bfloat16)
    return high, low


def places(cells):
    line = cells >> 7
    numbers = line & 255, ((line >> 8) << 7) + (cells & 127)
    return numbers


def hits(numbers, width):
    lines = lax.broadcasted_iota(jnp.int32, (256, width), 0)
    return lines == numbers


def narrow_hits(numbers, width):
    lines = lax.broadcasted_iota(jnp.int32, (256, width), 0)
    narrow = [n.astype(jnp.float32).astype(jnp.bfloat16) for n in (lines, numbers)]
    return narrow[0] == narrow[1]


def neighbours():
    lats, lons = lax.axis_size("lat"), lax.axis_size("lon")
    lat, lon = lax.axis_index("lat"), lax.axis_index("lon")
    steps = [(1, 0), (-1, 0), (0, 1), (0, -1), (1, 1), (1, -1), (-1, 1), (-1, -1)]
    return [(lax.rem(lat + a + lats, lats), lax.rem(lon + b + lons, lons)) for a, b in steps]


def swap_edges(field_ref, low_ref, high_ref, edges, send, receive):
    partners = neighbours()
    rows = field_ref.shape[1]
    top = field_ref.at[:, rows - EDGE : rows, :]
    bottom = field_ref.at[:, 0:EDGE, :]
    sources = [top, bottom, high_ref, low_ref, top, top, bottom, bottom]
    landing = [1, 0, 3, 2, 7, 6, 5, 4]
    copies = []
    for number in (0, 1, 4, 5, 6, 7, 2, 3):
        partner = partners[number]
        copy = pltpu.make_async_remote_copy(
            src_ref=sources[number],
            dst_ref=edges.at[landing[number]],
            send_sem=send.at[number],
            recv_sem=receive.at[landing[number]],
            device_id=partner,
            device_id_type=MESH,
        )
        copy.start()
        copies.append(copy)
    return copies


def assemble(level, field_ref, edges):
    shape = (EDGE, field_ref.shape[2])
    lane = lax.broadcasted_iota(jnp.int32, shape, 1)

    def corner(east, west):
        inner = jnp.where(lane >= shape[1] - EDGE, edges[west, level], 0.0)
        return jnp.where(lane < EDGE, edges[east, level], inner)

    gap = jnp.zeros((shape[1] - 2 * EDGE, field_ref.shape[1]), jnp.float32)
    beside = jnp.concatenate([edges[2, level], gap, edges[3, level]], 0).T
    upper = jnp.concatenate([field_ref[level], beside], 1)
    north = jnp.concatenate([edges[0, level], corner(4, 5)], 1)
    south = jnp.concatenate([edges[1, level], corner(6, 7)], 1)
    return jnp.concatenate([upper, north, south], 0)


def build_faces(stacked_ref, edges, out_ref):
    levels = out_ref.shape[1]
    rows, columns = out_ref.shape[2:]
    tile_rows = stacked_ref.shape[1]
    line = lax.broadcasted_iota(jnp.int32, (rows, columns), 0)
    line = jnp.where(line < tile_rows + EDGE, line, line - tile_rows - 2 * EDGE)
    line = lax.axis_index("lat") * tile_rows + line
    inside = (line >= 0) & (line < tile_rows * lax.axis_size("lat"))

    def per_level(level, carry):
        land = jnp.where(inside, assemble(level, stacked_ref, edges), 0.0)
        east = assemble(levels + level, stacked_ref, edges)
        north = assemble(2 * levels + level, stacked_ref, edges)
        east = east * land * pltpu.roll(land, columns - 1, 1)
        north = north * land * pltpu.roll(land, rows - 1, 0)
        out_ref[0, level] = east
        out_ref[1, level] = pltpu.roll(east, 1, 1)
        out_ref[2, level] = north
        out_ref[3, level] = pltpu.roll(north, 1, 0)
        return carry

    lax.fori_loop(0, levels, per_level, 0)


def edge_scratch(levels, columns):
    return [
        pltpu.VMEM((8, levels, EDGE, columns), jnp.float32),
        pltpu.SemaphoreType.DMA((8,)),
        pltpu.SemaphoreType.DMA((8,)),
    ]


def remote(number):
    return pltpu.CompilerParams(
        vmem_limit_bytes=48 * 1024 * 1024, collective_id=number, has_side_effects=True
    )


def everyone():
    lats, lons = lax.axis_size("lat"), lax.axis_size("lon")
    return lats * lons, lax.axis_index("lat") * lons + lax.axis_index("lon")


def where_is(device):
    lons = lax.axis_size("lon")
    return lax.div(device, lons), lax.rem(device, lons)


def greet_everyone():
    devices, me = everyone()
    barrier = pltpu.get_barrier_semaphore()

    def greet(distance, carry):
        partner = where_is(lax.rem(me + distance, devices))
        pl.semaphore_signal(barrier, inc=1, device_id=partner, device_id_type=MESH)
        return carry

    lax.fori_loop(1, devices, greet, 0)
    return barrier


def push(source, target, send, receive, device):
    pltpu.make_async_remote_copy(
        src_ref=source,
        dst_ref=target,
        send_sem=send,
        recv_sem=receive,
        device_id=where_is(device),
        device_id_type=MESH,
    ).start()


def wait_for(ref, semaphore):
    pltpu.make_async_copy(ref, ref, semaphore).wait()


def gather_and_send(here, field_ref, turned, found_ref, back, send, receive):
    square = jnp.concatenate([field_ref[0:256], field_ref[256:512]], 1).T
    high, low = split(square)
    turned[0:256] = high
    turned[256:512] = low
    devices, me = everyone()
    ranks, width = here.shape[1:]
    batch = GROUP // ranks
    groups = devices // batch
    zero, one = jnp.bfloat16(0), jnp.bfloat16(1)

    def group_of(turn):
        return lax.rem(lax.div(me, batch) + turn, groups)

    def send_group(turn):
        for item in range(batch):
            device = group_of(turn) * batch + item

            @pl.when(device != me)
            def _():
                push(found_ref.at[device], back.at[me], send, receive, device)

            @pl.when(device == me)
            def _():
                pltpu.make_async_copy(found_ref.at[device], back.at[device], receive).start()

    def step(turn, carry):
        start = group_of(turn) * batch
        places_of = [
            places(here[start + item // ranks, item % ranks : item % ranks + 1])
            for item in range(GROUP)
        ]
        right = [
            jnp.where(narrow_hits(row, width), one, zero) for row, _ in places_of
        ]
        found = jnp.dot(
            turned[...], jnp.concatenate(right, 1), preferred_element_type=jnp.float32
        )
        found = found[0:256] + found[256:512]
        for item in range(GROUP):
            part = found[:, item * width : (item + 1) * width]
            part = jnp.where(hits(places_of[item][1], width), part, 0.0)
            spot = item % ranks
            found_ref[start + item // ranks, spot : spot + 1] = jnp.sum(part, 0, keepdims=True)

        @pl.when(turn > 0)
        def _():
            send_group(turn - 1)

        return carry

    lax.fori_loop(0, groups, step, 0)
    send_group(groups - 1)
    wait_for(back, receive)


def weigh(turned, weights_ref, weighted):
    held = turned.shape[1]

    def step(number, carry):
        values = turned[...]
        start = pl.multiple_of(number * STEP, STEP)
        rows = []
        for item in range(STEP):
            column = values[:, item : item + 1]
            rows.append(jnp.sum(weights_ref[start + item] * column, 0, keepdims=True))
        weighted[pl.ds(start, STEP), :] = jnp.concatenate(rows, 0)
        turned[...] = pltpu.roll(values, held - STEP, 1)
        return carry

    lax.fori_loop(0, held // STEP, step, 0)


def scatter_arrivals(first, here, parcel, arrived, total, send, receive, between):
    devices, me = everyone()
    ranks, width = here.shape[1:]
    batch = GROUP // ranks
    groups = devices // batch
    mine = lax.div(me, batch)
    zero, one = jnp.bfloat16(0), jnp.bfloat16(1)

    pltpu.make_async_copy(parcel.at[me], arrived.at[me], receive.at[mine]).start()

    def tell(distance, carry):
        device = lax.rem(me + distance, devices)
        push(parcel.at[device], arrived.at[me], send, receive.at[mine], device)
        return carry

    lax.fori_loop(1, devices, tell, 0)
    between()

    def step(turn, carry):
        group = lax.rem(mine + 2 * groups - 1 - turn, groups)
        start = group * batch
        wait_for(arrived.at[pl.ds(start, batch)], receive.at[group])
        left, right = [], []
        for item in range(GROUP):
            device, spot = start + item // ranks, item % ranks
            if first:
                cells = arrived[device, spot : spot + 1].astype(jnp.int32)
                here[device, spot : spot + 1] = cells
                value = arrived[device, ranks + spot : ranks + spot + 1]
            else:
                cells = here[device, spot : spot + 1]
                value = arrived[device, spot : spot + 1]
            row, column = places(cells)
            row_hit = narrow_hits(row, width)
            left.append(jnp.concatenate([jnp.where(row_hit, part, zero) for part in split(value)], 0))
            right.append(jnp.where(narrow_hits(column, width), one, zero))
        total[...] += lax.dot_general(
            jnp.concatenate(left, 1),
            jnp.concatenate(right, 1),
            (((1,), (1,)), ((), ())),
            preferred_element_type=jnp.float32,
        )
        return carry

    lax.fori_loop(0, groups, step, 0)


def phase(mode, place_ref, weights_ref, sigma_ref, faces_ref, here, common, sparse, more):
    first, last = mode == "first", mode == "last"
    turned, weighted, total, field_ref, low, high, work = common[:7]
    send, receive, edges, edge_send, edge_receive = common[7:12]
    parcel, arrived = sparse[:2]
    if first:
        cells_ref, value_ref, ready, smoothed, field_out, stacked = more
    else:
        square, found, back, found_send, found_receive = sparse[2:]
    if last:
        seen_ref, base_ref, once_ref, base_seen_ref, smoothed, increment = more[:6]
        part, parts, part_send, part_receive = more[6:]
    elif not first:
        seen_ref, smoothed, field_out = more
    devices, me = everyone()
    ranks, width = here.shape[1:]
    held = turned.shape[1]
    number = lax.broadcasted_iota(jnp.int32, (devices, held), 0)

    def placing(rank):
        return jnp.where(number * ranks + rank == place_ref[0:1], 1.0, 0.0)

    stacked_copies = []
    if first:
        stacked_copies = swap_edges(*stacked)
        turned[...] = value_ref[...].T
    else:
        gather_and_send(here, seen_ref, square, found, back, found_send, found_receive)
        turned[...] = sum(
            lax.dot_general(
                back[:, rank, :],
                placing(rank),
                (((0,), (0,)), ((), ())),
                precision=EXACT,
                preferred_element_type=jnp.float32,
            )
            for rank in range(ranks)
        )
    if first:
        ready()
    weigh(turned, weights_ref, weighted)
    for rank in range(ranks):
        chosen = placing(rank)
        if first:
            parcel[:, rank, :] = jnp.dot(
                chosen,
                cells_ref[...].astype(jnp.float32),
                precision=EXACT,
                preferred_element_type=jnp.float32,
            )
        parcel[:, (ranks if first else 0) + rank, :] = jnp.dot(
            chosen, weighted[...], precision=EXACT, preferred_element_type=jnp.float32
        )
    total[...] = jnp.zeros_like(total)

    def between():
        if first:
            for copy in stacked_copies:
                copy.wait()
            build_faces(stacked[0], stacked[3], faces_ref)

    scatter_arrivals(first, here, parcel, arrived, total, send, receive, between)

    field = total[0:256] + total[256:512]
    levels, tile_rows, tile_columns = field_ref.shape
    for level in range(levels):
        start, side = level * 128 % 256, level * 128 // 256 * 128
        tile = field[start : start + 128, side : side + 128] * sigma_ref[level]
        field_ref[level] = tile
        flat = tile.T
        low[level] = flat[0:EDGE]
        high[level] = flat[tile_columns - EDGE :]
    copies = swap_edges(field_ref, low, high, edges, edge_send, edge_receive)
    for copy in copies:
        copy.wait()
    rows, columns = work.shape[1:]

    def one_pass(level, x):
        result = x + faces_ref[0, level] * (pltpu.roll(x, columns - 1, 1) - x)
        result += faces_ref[1, level] * (pltpu.roll(x, 1, 1) - x)
        result += faces_ref[2, level] * (pltpu.roll(x, rows - 1, 0) - x)
        result += faces_ref[3, level] * (pltpu.roll(x, 1, 0) - x)
        work[level] = result

    def per_level(level, carry):
        one_pass(level, assemble(level, field_ref, edges))
        for sweep in range(PASSES - 1):
            one_pass(level, work[level])
        tile = work[level, 0:tile_rows, 0:tile_columns]
        smoothed[level] = tile
        if not last:
            for sweep in range(PASSES):
                one_pass(level, work[level])
            tile = work[level, 0:tile_rows, 0:tile_columns]
            start = pl.multiple_of(level * tile_rows, tile_rows)
            field_out[pl.ds(start, tile_rows), :] = sigma_ref[level] * tile
            return carry
        base, once = base_ref[level], once_ref[level]
        products = (base * base, base * once, once * once, once * tile)
        return tuple(c + jnp.sum(p, 0, keepdims=True) for c, p in zip(carry, products))

    sums = tuple(jnp.zeros((1, tile_columns), jnp.float32) for _ in range(4))
    sums = lax.fori_loop(0, levels, per_level, sums)
    if last:
        lane = lax.broadcasted_iota(jnp.int32, (1, tile_columns), 1)
        row = jnp.zeros((1, tile_columns), jnp.float32)
        for spot in range(4):
            row = jnp.where(lane == spot, jnp.sum(sums[spot], 1, keepdims=True), row)
        part[...] = row
        wait_for(arrived.at[pl.ds(0, devices - 1)], send)
        wait_for(back.at[pl.ds(0, devices - 1)], found_send)

        def tell(distance, carry):
            device = lax.rem(me + distance, devices)
            push(part, parts.at[distance - 1], part_send, part_receive, device)
            return carry

        lax.fori_loop(1, devices, tell, 0)
        wait_for(parts, part_receive)
        row = row + jnp.sum(parts[...], 0)
        s0, s1, s2, s3 = (
            jnp.sum(jnp.where(lane == spot, row, 0.0), 1, keepdims=True) for spot in range(4)
        )
        alpha = s0 / (s0 + s1)
        rest = s1 / (s0 + s1)
        norm = alpha * (alpha * s2 - rest * s1)
        along = rest + norm / s0
        norm_next = along * along * s0 - 2 * along * alpha * s1 + alpha * alpha * s2
        energy = along * along * s1 - 2 * along * alpha * s2 + alpha * alpha * s3
        step = norm / (norm_next + energy)
        scales = [
            alpha + step * along,
            step * alpha,
            rest - step * along,
            step * alpha - alpha - step * along,
        ]
        for level in range(levels):
            flat = slice(level * tile_rows, (level + 1) * tile_rows)
            increment[level] = scales[0] * base_seen_ref[flat] - scales[1] * seen_ref[flat]
            smoothed[level] = (
                scales[2] * base_ref[level]
                + scales[3] * once_ref[level]
                + scales[1] * smoothed[level]
            )
        wait_for(parts, part_send)
    else:
        wait_for(arrived.at[pl.ds(0, devices - 1)], send)
        if not first:
            wait_for(back.at[pl.ds(0, devices - 1)], found_send)


def kernel(*refs):
    place_ref, weights_hbm, sigma_ref, cells_ref, value_ref, mask_ref, east_ref, north_ref = refs[:8]
    increment, residual = refs[8:10]
    base, once, base_field, once_field, here, faces_ref, weights_ref, copied = refs[10:18]
    common, wide, narrow = refs[18:30], refs[30:32], refs[32:39]
    stacked, finish = refs[39:45], refs[45:]
    load = pltpu.make_async_copy(weights_hbm, weights_ref, copied)
    load.start()
    barrier = greet_everyone()
    fields, low, high = stacked[:3]
    levels, rows, columns = sigma_ref.shape
    for kind, ref in enumerate((mask_ref, east_ref, north_ref)):
        for level in range(levels):
            tile = ref[level].astype(jnp.float32)
            flat = tile.T
            fields[kind * levels + level] = tile
            low[kind * levels + level] = flat[0:EDGE]
            high[kind * levels + level] = flat[columns - EDGE :]
    pl.semaphore_wait(barrier, everyone()[0] - 1)
    fixed = (place_ref, weights_ref, sigma_ref, faces_ref, here, common)
    phase("first", *fixed, wide, (cells_ref, value_ref, load.wait, base, base_field, stacked))
    phase("middle", *fixed, narrow, (base_field, once, once_field))
    phase(
        "last",
        *fixed,
        narrow,
        (once_field, base, once, base_field, residual, increment) + finish,
    )


def body(sigma, east_coef, north_coef, mask, innovations, cells, owner, obs_weights):
    held, width = cells.shape
    devices = lax.axis_size("lat") * lax.axis_size("lon")
    levels, rows, columns = sigma.shape
    target = owner[:, 0]
    order = jnp.arange(held, dtype=jnp.int32)
    before = (target[:, None] == target[None, :]) & (order[:, None] < order[None, :])
    rank = jnp.sum(before.astype(jnp.int32), axis=0)
    place = jnp.stack([target * 2 + rank] * 8)
    real = jnp.float32
    dma = pltpu.SemaphoreType.DMA
    padded = (levels, rows + 2 * EDGE, 2 * columns)
    tile = pltpu.VMEM(sigma.shape, real)
    flat = pltpu.VMEM((levels * rows, columns), real)
    parcel = pltpu.VMEM((devices, 2, width), real)
    twice = pltpu.VMEM((devices, 4, width), real)
    strip = pltpu.VMEM((levels, EDGE, rows), real)
    strips = pltpu.VMEM((3 * levels, EDGE, rows), real)
    scratch = [tile, tile, flat, flat, pltpu.VMEM((devices, 2, width), jnp.int32)]
    scratch += [pltpu.VMEM((4,) + padded, real), pltpu.VMEM(obs_weights.shape, real), dma]
    scratch += [
        pltpu.VMEM((width, held), real),
        pltpu.VMEM((held, width), real),
        pltpu.VMEM((512, 256), real),
        tile,
        strip,
        strip,
        pltpu.VMEM(padded, real),
        dma,
        dma((devices * 2 // GROUP,)),
    ] + edge_scratch(levels, columns)
    scratch += [twice, twice]
    scratch += [parcel, parcel, pltpu.VMEM((512, 256), jnp.bfloat16), parcel, parcel, dma, dma]
    scratch += [pltpu.VMEM((3 * levels, rows, columns), real), strips, strips]
    scratch += edge_scratch(3 * levels, columns)
    scratch += [
        pltpu.VMEM((1, columns), real),
        pltpu.VMEM((devices - 1, 1, columns), real),
        dma,
        dma,
    ]
    specs = [VMEM] * 8
    specs[1] = pl.BlockSpec(memory_space=pl.ANY)
    out = jax.ShapeDtypeStruct(sigma.shape, real)
    return pl.pallas_call(
        kernel,
        out_shape=(out, out),
        in_specs=specs,
        out_specs=(VMEM, VMEM),
        scratch_shapes=scratch,
        compiler_params=remote(1),
        name="whole",
    )(place, obs_weights, sigma, cells, innovations, mask, east_coef, north_coef)


def solution(mesh):
    return jax.shard_map(
        body,
        mesh=mesh,
        in_specs=(
            P(None, "lat", "lon"),
            P(None, "lat", "lon"),
            P(None, "lat", "lon"),
            P(None, "lat", "lon"),
            P(("lat", "lon"), None),
            P(("lat", "lon"), None),
            P(("lat", "lon"), None),
            P(("lat", "lon"), None, None),
        ),
        out_specs=(P(None, "lat", "lon"), P(None, "lat", "lon")),
        check_vma=False,
    )
```
